32 devices in a mesh: expo: 4 (over y, x), fp: 8 (over z, core).
Axes of the slice: x: 2, y: 2, z: 4, core: 2. Of those that a mesh axis runs over, the one named last changes fastest.
Arguments:
- raw_pixels: bfloat16 [4, 2048, 2048], P('expo', 'fp'), may hold values from -6 to 6
- kernel_bank: bfloat16 [8, 2, 41], replicated, may hold values from -1 to 1
- kernel_ids: int32 [4, 8], P('expo', 'fp'), may hold values from 0 to 7
- inv_var: float32 [4, 8], P('expo', 'fp'), may hold values from 0.3 to 3
- gap_start: int32 [4, 8], P('expo', 'fp'), may hold values from 0 to 224
- warp_tile: int32 [4, 2048, 16, 1], P('expo', 'fp'), may hold values from 0 to 31; in each aligned block of 4096 rows (0 to 4095, 4096 to 8191, ..., all dimensions but the last counted through in order) at most 256 rows name the same one
- warp_offset: int32 [4, 2048, 16], P('expo', 'fp'), may hold values from 0 to 4095
Outputs:
- coadd_image: float32 [32, 4096, 128], P(('expo', 'fp'))
- coadd_weight: float32 [32, 4096], P(('expo', 'fp'))
The draws below stay inside these ranges and needn't reach their ends.
Inputs may be any that keep to these rules, and one draw needn't show every extreme that they name: `warp_tile`: among the 4096 row segments of one exposure's CCD window (256 pixel rows of 16 segments each), at most 256 go to one tile, and in some windows exactly 256 do.
All inputs are finite; a program needn't handle non-finite values.
Results may differ from the reference program's by a relative error of at most 0.006.
Values may be sent and summed in bfloat16 or wider, within the bound.
No kernel may reach another device: no remote copies, remote signals or barrier semaphores. Data moves between devices by JAX's collectives and lax.ppermute only.
A program may use at most 64 MiB of HBM per device.

```python
import math
import jax
import jax.numpy as jnp
import numpy as np
from jax import lax

ROWS = 256
COLS = 2048
TAPS = 41
SEG = 128
KBANK = 8
GAP = 32
EXPOSURES = 4
NROWS = 2048
SEGS = 16
TILES = 32
TILE_SLOTS = 4096
CAP = 256
N_FP = 8


def touch_ends(array, own_key, least, high):
    extent = array.shape
    spot = [jax.random.randint(jax.random.fold_in(own_key, axis), (), 0, extent[axis]) for axis in range(len(extent))]
    array = array.at[tuple(spot)].set(least)
    longest = extent.index(max(extent))
    spot[longest] = (spot[longest] + 1) % extent[longest]
    return array.at[tuple(spot)].set(high)


def steps_of(stream_key, shape, cuts, low, largest):
    def one(axis_at, parts):
        draws = jax.random.uniform(jax.random.fold_in(jax.random.fold_in(stream_key, 6), axis_at), (parts,), jnp.float32, low / len(cuts), largest / len(cuts))
        return jnp.repeat(jnp.exp(draws), shape[axis_at] // parts).reshape((-1,) + (1,) * (len(shape) - axis_at - 1))

    level = one(*cuts[0])
    for cut in cuts[1:]:
        level = level * one(*cut)
    return level


def deal_out(own_key, own, number, rows, number_of, top, most, lean):
    sequence = jax.random.permutation(own_key, number_of)
    heavy_load, usual = portions_of(number_of, rows * top, most, lean, True), portions_of(number_of, rows * top, most, lean, False)
    places = jnp.arange(number_of)

    def named(lengths, turn):
        used = int((lengths > 0).sum())
        fixed = max(1, used // 4)
        passed = fixed + (places - fixed + turn * (used - fixed)) % max(1, number_of - fixed)
        return jnp.zeros((number_of,), jnp.int32).at[sequence[jnp.where(places < fixed, places, passed)]].set(jnp.asarray(lengths, jnp.int32))

    lengths = jnp.where(number % 4 == 0, named(heavy_load, number // 4), named(usual, number - number // 4 - 1))
    mixed = jax.random.permutation(jax.random.fold_in(own, 3), number_of)
    giver, sink = mixed[0:number_of // 2 * 2:2], mixed[1:number_of // 2 * 2:2]
    margin = jnp.minimum(lengths[giver] - 1, most - lengths[sink]) // 2
    margin = jnp.where((giver == sequence[0]) | (sink == sequence[0]) | (lengths[sink] == 0), 0, jnp.maximum(margin, 0))
    passed = jax.random.randint(jax.random.fold_in(own, 4), (number_of // 2,), 0, 1 << 20) % (margin + 1)
    lengths = lengths.at[giver].add(-passed).at[sink].add(passed)
    labels = jnp.searchsorted(jnp.cumsum(lengths), jnp.arange(rows * top), side="right").astype(jnp.int32)
    grid = labels.reshape(top, rows).T
    grid = grid[jax.random.permutation(jax.random.fold_in(own, 1), rows)]
    turn = jax.random.randint(jax.random.fold_in(own, 2), (rows, 1), 0, top)
    return jnp.take_along_axis(grid, (jnp.arange(top)[None, :] + turn) % top, axis=1)


def portions_of(amount, total, reach, lean, full):
    loads = [(1 << 20) // math.isqrt(standing ** lean) + 1 for standing in range(1, amount + 1)]
    largest = reach if full else min(reach, max(-(-total // amount), total * loads[0] // sum(loads)))
    least = 1 if total - largest >= amount - 1 else 0
    given, rest = [largest] + [least] * (amount - 1), total - largest - least * (amount - 1)
    while rest > 0:
        candidates = [i for i in range(1, amount) if given[i] < largest] or [i for i in range(1, amount) if given[i] < reach]
        whole, left = sum([loads[i] for i in candidates]), rest
        for i in candidates:
            addition = min(reach - given[i], max(1, left * loads[i] // whole), rest)
            given[i] = given[i] + addition
            rest = rest - addition
    return np.array(given)


def scatter_about(key, dims, scale, bound, cuts=(), held_as=jnp.bfloat16):
    drawn = scale * jax.random.normal(key, dims, jnp.float32)
    if cuts:
        drawn = drawn * steps_of(key, dims, cuts, -0.22, 0.18)
    return jnp.clip(drawn, -bound, bound).astype(held_as)


def setup_inputs(seed: int = 0) -> dict:
    splits = jax.random.split(jax.random.key(seed), 8)
    raw_pixels = scatter_about(splits[0], (EXPOSURES, NROWS, COLS), 1.0, 6.0, ((0, 4), (1, 8)))
    kernel_bank = scatter_about(splits[1], (KBANK, 2, TAPS), 0.15625, 1.0)
    kernel_ids = touch_ends(jax.random.randint(splits[2], (EXPOSURES, N_FP), 0, KBANK), jax.random.fold_in(splits[2], 1), 0, KBANK - 1).astype(jnp.int32)
    inv_var = jnp.clip(jnp.exp(math.log(3.0) - 2.3025851 * jax.random.uniform(splits[3], (EXPOSURES, N_FP), jnp.float32) ** steps_of(splits[3], (EXPOSURES, N_FP), ((0, 4), (1, 8)), -0.2, 0.2)), 0.3, 3.0)
    gap_start = touch_ends(jax.random.randint(splits[4], (EXPOSURES, N_FP), 0, ROWS - GAP + 1), jax.random.fold_in(splits[4], 1), 0, ROWS - GAP).astype(jnp.int32)
    warp_tile_keys = jax.random.split(jax.random.fold_in(splits[5], 1), EXPOSURES * NROWS * SEGS // (ROWS * SEGS))
    warp_tile_turns = jax.random.permutation(jax.random.fold_in(splits[5], 3), EXPOSURES * NROWS * SEGS // (ROWS * SEGS))
    warp_tile = jax.vmap(lambda own, number: deal_out(jax.random.fold_in(splits[5], 2), own, number, ROWS * SEGS, TILES, 1, CAP, 2))(warp_tile_keys, warp_tile_turns).reshape((EXPOSURES, NROWS, SEGS, 1))
    warp_offset = touch_ends(jax.random.randint(splits[6], (EXPOSURES, NROWS, SEGS), 0, TILE_SLOTS), jax.random.fold_in(splits[6], 1), 0, TILE_SLOTS - 1).astype(jnp.int32)
    return dict(raw_pixels=raw_pixels, kernel_bank=kernel_bank, kernel_ids=kernel_ids, inv_var=inv_var, gap_start=gap_start, warp_tile=warp_tile, warp_offset=warp_offset)


def pass_rows(frame_pixels, tap_rows):
    half_taps = tap_rows.shape[1] // 2
    padded = jnp.pad(frame_pixels.astype(jnp.float32), ((half_taps, half_taps), (0, 0)))
    running_sum = jnp.zeros(frame_pixels.shape, jnp.float32)
    for tap_index in range(tap_rows.shape[1]):
        running_sum = running_sum + tap_rows[:, tap_index:tap_index + 1].astype(jnp.float32) * padded[tap_index:tap_index + frame_pixels.shape[0]]
    return running_sum


def pass_columns(frame_pixels, tap_rows):
    half_taps = tap_rows.shape[1] // 2
    padded = jnp.pad(frame_pixels, ((0, 0), (half_taps, half_taps)))
    running_sum = jnp.zeros(frame_pixels.shape, jnp.float32)
    for tap_index in range(tap_rows.shape[1]):
        running_sum = running_sum + tap_rows[:, tap_index:tap_index + 1].astype(jnp.float32) * padded[:, tap_index:tap_index + frame_pixels.shape[1]]
    return running_sum


def reference(raw_pixels, kernel_bank, kernel_ids, inv_var, gap_start, warp_tile, warp_offset):
    slots_all = TILES * TILE_SLOTS
    row_local = jnp.arange(NROWS) % ROWS

    def exposure(running, inputs):
        frame_pixels, ids_row, weight_row, gap_row, tile_row, offset_row = inputs
        vertical_taps = jnp.repeat(kernel_bank[ids_row, 0], ROWS, axis=0)
        horizontal_taps = jnp.repeat(kernel_bank[ids_row, 1], ROWS, axis=0)
        vertical = pass_rows(frame_pixels, vertical_taps)
        vertical = lax.optimization_barrier(vertical.astype(jnp.bfloat16)).astype(jnp.float32)
        convolved = pass_columns(vertical, horizontal_taps)
        convolved = lax.optimization_barrier(convolved.astype(jnp.bfloat16)).astype(jnp.float32)
        gap_rows = jnp.repeat(gap_row, ROWS)
        in_gap = (row_local >= gap_rows) & (row_local < gap_rows + GAP)
        row_weight = jnp.where(in_gap, jnp.zeros_like(weight_row[0]), jnp.repeat(weight_row, ROWS))
        piece_weight = jnp.repeat(row_weight, SEGS)
        pieces = convolved.reshape(NROWS * SEGS, SEG)
        slot_ids = (tile_row.reshape(-1).astype(jnp.int32) * TILE_SLOTS + offset_row.reshape(-1).astype(jnp.int32)).astype(jnp.int32)
        weighted_sum, weight_sum = running
        weighted_sum = weighted_sum + jax.ops.segment_sum(piece_weight[:, None] * pieces, slot_ids, num_segments=slots_all)
        weight_sum = weight_sum + jax.ops.segment_sum(piece_weight, slot_ids, num_segments=slots_all)
        return (weighted_sum, weight_sum), None

    initial = (jnp.zeros((slots_all, SEG), jnp.float32), jnp.zeros((slots_all,), jnp.float32))
    (weighted_sum, weight_sum), ignored = lax.scan(exposure, initial, (raw_pixels, kernel_ids, inv_var, gap_start, warp_tile, warp_offset))
    coadd_image = weighted_sum / jnp.maximum(weight_sum, 1.0)[:, None]
    return coadd_image.reshape(TILES, TILE_SLOTS, SEG), weight_sum.reshape(TILES, TILE_SLOTS)
```

```python
import functools

import jax
import jax.numpy as jnp
from jax import lax
from jax.experimental import pallas as pl
from jax.experimental.pallas import tpu as pltpu
from jax.sharding import PartitionSpec as P

GAP = 32
EDGE = 32
LANES = 128
SPLIT = 4

VMEM = pl.BlockSpec(memory_space=pltpu.VMEM)
SMEM = pl.BlockSpec(memory_space=pltpu.SMEM)
ANY = pl.BlockSpec(memory_space=pl.ANY)


def iota(shape, dim):
    return lax.broadcasted_iota(jnp.int32, shape, dim)


def dot_last(a, b):
    return lax.dot_general(a, b, (((1,), (1,)), ((), ())), preferred_element_type=jnp.float32)


def halo(shard, axis):
    size = lax.axis_size(axis)
    up = [(i, i + 1) for i in range(size - 1)]
    down = [(i + 1, i) for i in range(size - 1)]
    above = lax.ppermute(shard[-EDGE:], axis, up)
    below = lax.ppermute(shard[:EDGE], axis, down)
    return above, below


def route_kernel(half, tile_ref, off_ref, gap_ref, var_ref, id_ref, bank_ref, dest_ref, meta_ref, tv_ref, th_ref):
    segs, rows = off_ref.shape
    devices = meta_ref.shape[0]
    capacity = meta_ref.shape[1] - LANES
    taps = bank_ref[id_ref[0, 0]]
    for ref, which, shift in ((tv_ref, 0, EDGE - half), (th_ref, 1, LANES - half)):
        height, width = ref.shape
        line = jnp.concatenate([taps[which : which + 1, :]] + [jnp.zeros((1, LANES), jnp.float32)] * (width // LANES - 1), axis=1)
        wide = jnp.broadcast_to(line, (height, width))
        ref[...] = pltpu.roll(wide, shift // 8 * 8, 1, stride=1, stride_axis=0).astype(jnp.bfloat16)
    gap = gap_ref[0, 0]
    line = iota((1, rows), 1)
    kept = jnp.logical_or(line < gap, line >= gap + GAP)
    before = (iota((rows, rows), 0) < iota((rows, rows), 1)).astype(jnp.bfloat16)
    owner = iota((devices, rows), 0)
    place = iota((capacity, rows), 0)
    base = jnp.zeros((devices, 1), jnp.float32)
    packed = jnp.zeros((3 * devices, capacity), jnp.float32)
    for s in range(segs):
        tile = jnp.where(kept, tile_ref[s], -1)
        hot = tile == owner
        hot_value = hot.astype(jnp.float32)
        hot_low = hot_value.astype(jnp.bfloat16)
        prefix = jnp.dot(hot_low, before, preferred_element_type=jnp.float32)
        rank = jnp.sum(hot_value * (prefix + base), axis=0, keepdims=True).astype(jnp.int32)
        base = base + jnp.sum(hot_value, axis=1, keepdims=True)
        dest_ref[s : s + 1, :] = jnp.where(kept, tile * capacity + rank, devices * capacity)
        spot = (place == rank).astype(jnp.bfloat16)
        offset = off_ref[s : s + 1, :]
        high = (offset >> 6).astype(jnp.float32)
        low = (offset & 63).astype(jnp.float32)
        stack = jnp.concatenate([hot_value * high, hot_value * low, hot_value], axis=0).astype(jnp.bfloat16)
        packed = packed + dot_last(stack, spot)
    found = packed[2 * devices :] > 0.5
    offsets = packed[:devices] * 64.0 + packed[devices : 2 * devices]
    meta_ref[:, :capacity] = jnp.where(found, offsets, -1.0)
    meta_ref[:, capacity:] = jnp.full((devices, LANES), var_ref[0, 0], jnp.float32)


def pack_kernel(raw_ref, above_ref, below_ref, tv_ref, th_ref, dest_ref, out_ref, edged, vert, conv, spread, sems):
    rows, cols = raw_ref.shape
    segs = cols // LANES
    copies = [
        pltpu.make_async_copy(above_ref, edged.at[pl.ds(0, EDGE)], sems.at[0]),
        pltpu.make_async_copy(raw_ref, edged.at[pl.ds(EDGE, rows)], sems.at[1]),
        pltpu.make_async_copy(below_ref, edged.at[pl.ds(EDGE + rows, EDGE)], sems.at[2]),
    ]
    for copy in copies:
        copy.start()
    vert[:, :LANES] = jnp.zeros((rows, LANES), jnp.bfloat16)
    vert[:, LANES + cols :] = jnp.zeros((rows, LANES), jnp.bfloat16)
    for copy in copies:
        copy.wait()
    wide = 2 * LANES
    tall = rows + 2 * EDGE
    for c in range(cols // wide):
        part = jnp.dot(tv_ref[:, :tall], edged[:, c * wide : (c + 1) * wide], preferred_element_type=jnp.float32)
        vert[:, LANES + c * wide : LANES + (c + 1) * wide] = part.astype(jnp.bfloat16)
    for c in range(cols // wide):
        part = dot_last(vert[:, c * wide : c * wide + 2 * wide], th_ref[...])
        conv[2 * c * rows : (2 * c + 1) * rows, :] = part[:, :LANES]
        conv[(2 * c + 1) * rows : (2 * c + 2) * rows, :] = part[:, LANES:]

    group = 32

    def scatter(step, carry):
        start = pl.multiple_of(step * group, group)
        for j in range(group):
            spot = dest_ref[start + j]
            spread[pl.ds(spot, 1), :] = conv[pl.ds(start + j, 1), :]
        return carry

    lax.fori_loop(0, segs * rows // group, scatter, 0)

    devices, capacity, _ = out_ref.shape

    def emit(step, carry):
        start = pl.multiple_of(step * capacity, capacity)
        out_ref[step] = spread[pl.ds(start, capacity), :].astype(jnp.bfloat16)
        return carry

    lax.fori_loop(0, devices, emit, 0)


def sum_kernel(values_ref, meta_ref, off_ref, var_ref, image_ref, weight_ref, scaled, *sums):
    devices, capacity, _ = values_ref.shape
    slots = image_ref.shape[0]
    high_rows = slots // LANES

    def clear(step, carry):
        start = pl.multiple_of(step * 64, 64)
        for acc in sums:
            acc[pl.ds(start, 64), :] = jnp.zeros((64, LANES), jnp.float32)
        return carry

    lax.fori_loop(0, slots // 64, clear, 0)

    high_id = iota((high_rows, capacity), 0)
    low_id = iota((LANES, capacity), 0)

    def source(src, weight):
        factor = var_ref[src]
        scaled[...] = values_ref[src].astype(jnp.float32) * factor
        offset = meta_ref[src, :, :capacity].astype(jnp.int32)
        high = ((offset >> 7) == high_id).astype(jnp.bfloat16)
        low = ((offset & 127) == low_id).astype(jnp.bfloat16)
        count = dot_last(high, low)

        group = 32

        def add(step, carry):
            start = pl.multiple_of(step * group, group)
            for j in range(0, group, len(sums)):
                spots = [off_ref[src * capacity + start + j + k] for k in range(len(sums))]
                held = [acc[pl.ds(spot, 1), :] for acc, spot in zip(sums, spots)]
                fresh = [scaled[pl.ds(start + j + k, 1), :] for k in range(len(sums))]
                for acc, spot, one, two in zip(sums, spots, held, fresh):
                    acc[pl.ds(spot, 1), :] = one + two
            return carry

        lax.fori_loop(0, capacity // group, add, 0)
        return weight + factor * count

    weight = lax.fori_loop(0, devices, source, jnp.zeros((high_rows, LANES), jnp.float32))
    weight_ref[...] = weight
    for h in range(high_rows):
        scale = jnp.broadcast_to(jnp.maximum(weight[h : h + 1, :], 1.0), (LANES, LANES)).T
        total = sums[0][h * LANES : (h + 1) * LANES, :]
        for acc in sums[1:]:
            total = total + acc[h * LANES : (h + 1) * LANES, :]
        image_ref[h * LANES : (h + 1) * LANES, :] = total / scale


def body(raw_pixels, kernel_bank, kernel_ids, inv_var, gap_start, warp_tile, warp_offset):
    _, rows, cols = raw_pixels.shape
    segs = cols // LANES
    axes = ("expo", "fp")
    devices = lax.axis_size("expo") * lax.axis_size("fp")
    pieces = rows * segs
    capacity = 2 * pieces // devices
    slots = pieces
    f32, bf16, i32 = jnp.float32, jnp.bfloat16, jnp.int32

    raw = raw_pixels[0]
    above, below = halo(raw, "fp")
    tiles = jnp.transpose(warp_tile[0], (1, 2, 0))
    offsets = jnp.transpose(warp_offset[0], (1, 0))
    taps = kernel_bank.shape[2]
    lead = -(taps // 2) % 8
    bank = jnp.pad(kernel_bank.astype(f32), ((0, 0), (0, 0), (lead, LANES - taps - lead)))
    tall = -(-(rows + 2 * EDGE) // LANES) * LANES
    dest, meta, tv, th = pl.pallas_call(
        functools.partial(route_kernel, taps // 2),
        out_shape=(
            jax.ShapeDtypeStruct((segs, rows), i32),
            jax.ShapeDtypeStruct((devices, capacity + LANES), f32),
            jax.ShapeDtypeStruct((rows, tall), bf16),
            jax.ShapeDtypeStruct((2 * LANES, 4 * LANES), bf16),
        ),
        in_specs=[VMEM, VMEM, SMEM, SMEM, SMEM, VMEM],
        out_specs=(VMEM, VMEM, VMEM, VMEM),
        cost_estimate=pl.CostEstimate(flops=400_000_000, bytes_accessed=600_000, transcendentals=0),
        name="route",
    )(tiles, offsets, gap_start, inv_var, kernel_ids, bank)

    got_meta = lax.all_to_all(meta, axes, split_axis=0, concat_axis=0, tiled=True)

    send = pl.pallas_call(
        pack_kernel,
        out_shape=jax.ShapeDtypeStruct((devices, capacity, LANES), bf16),
        in_specs=[ANY, ANY, ANY, VMEM, VMEM, SMEM],
        out_specs=VMEM,
        scratch_shapes=[
            pltpu.VMEM((rows + 2 * EDGE, cols), bf16),
            pltpu.VMEM((rows, cols + 2 * LANES), bf16),
            pltpu.VMEM((pieces, LANES), f32),
            pltpu.VMEM((devices * capacity + 8, LANES), f32),
            pltpu.SemaphoreType.DMA((3,)),
        ],
        cost_estimate=pl.CostEstimate(flops=10_000_000_000, bytes_accessed=4_000_000, transcendentals=0),
        name="pack",
    )(raw, above, below, tv, th, dest.reshape(-1))

    got = lax.all_to_all(send, axes, split_axis=0, concat_axis=0, tiled=True)

    spots = got_meta[:, :capacity].astype(i32)
    spots = jnp.where(spots < 0, slots, spots).reshape(-1)
    factors = got_meta[:, capacity]
    image, weight = pl.pallas_call(
        sum_kernel,
        out_shape=(
            jax.ShapeDtypeStruct((slots, LANES), f32),
            jax.ShapeDtypeStruct((slots // LANES, LANES), f32),
        ),
        in_specs=[VMEM, VMEM, SMEM, SMEM],
        out_specs=(VMEM, VMEM),
        scratch_shapes=[pltpu.VMEM((capacity, LANES), f32)]
        + [pltpu.VMEM((slots + 8, LANES), f32) for _ in range(SPLIT)],
        cost_estimate=pl.CostEstimate(flops=10_000_000_000, bytes_accessed=4_000_000, transcendentals=0),
        name="sum",
    )(got, got_meta.reshape(devices, 1, -1), spots, factors)
    return image[None], weight.reshape(1, slots)


def solution(mesh):
    in_specs = (
        P("expo", "fp", None),
        P(),
        P("expo", "fp"),
        P("expo", "fp"),
        P("expo", "fp"),
        P("expo", "fp", None, None),
        P("expo", "fp", None),
    )
    out_specs = (P(("expo", "fp"), None, None), P(("expo", "fp"), None))
    return jax.shard_map(body, mesh=mesh, in_specs=in_specs, out_specs=out_specs, check_vma=False)
```

```python
import functools

import jax
import jax.numpy as jnp
from jax import lax
from jax.experimental import pallas as pl
from jax.experimental.pallas import tpu as pltpu
from jax.sharding import PartitionSpec as P

GAP = 32
EDGE = 32
LANES = 128
META = 8
SPLIT = (8, 4)
GROUP = 8

VMEM = pl.BlockSpec(memory_space=pltpu.VMEM)
ANY = pl.BlockSpec(memory_space=pl.ANY)
f32, bf16, i32 = jnp.float32, jnp.bfloat16, jnp.int32


def iota(shape, dim):
    return lax.broadcasted_iota(i32, shape, dim)


def dot_last(a, b):
    return lax.dot_general(a, b, (((1,), (1,)), ((), ())), preferred_element_type=f32)


def near(x):
    return pltpu.with_memory_space_constraint(x, pltpu.VMEM)


def far(x):
    return pltpu.with_memory_space_constraint(x, pltpu.HBM)


def params(mib):
    return pltpu.CompilerParams(vmem_limit_bytes=mib << 20)


def cost(flops, moved):
    return pl.CostEstimate(flops=flops, bytes_accessed=moved, transcendentals=0)


def halo(shard, axis):
    size = lax.axis_size(axis)
    up = [(i, i + 1) for i in range(size - 1)]
    down = [(i + 1, i) for i in range(size - 1)]
    above = lax.ppermute(shard[-EDGE:], axis, up)
    below = lax.ppermute(shard[:EDGE], axis, down)
    return above, below


def route_kernel(capacity, tile_ref, off_ref, gap_ref, var_ref, id_ref, bank_ref, dest_ref, meta_ref, tv_ref, th_ref, line_ref):
    segs, rows = off_ref.shape
    devices = meta_ref.shape[0] // META
    parts = -(-capacity // LANES)
    bank = bank_ref[...].astype(f32)
    chosen = jnp.where(id_ref[...] == 0, bank[0], 0.0)
    for k in range(1, bank.shape[0]):
        chosen = jnp.where(id_ref[...] == k, bank[k], chosen)
    taps = bank.shape[2]
    half = taps // 2
    lead = -half % 8
    line_ref[...] = jnp.zeros(line_ref.shape, f32)
    line_ref[:, lead : lead + taps] = chosen
    for ref, which, shift in ((tv_ref, 0, EDGE - half), (th_ref, 1, LANES - half)):
        height, width = ref.shape
        wide = jnp.broadcast_to(line_ref[which : which + 1, :width], (height, width))
        ref[...] = pltpu.roll(wide, shift - lead, 1, stride=1, stride_axis=0).astype(bf16)
    gap = gap_ref[...]
    line = iota((1, rows), 1)
    kept = jnp.logical_or(line < gap, line >= gap + GAP)
    before = (iota((rows, rows), 0) < iota((rows, rows), 1)).astype(bf16)
    owner = iota((devices, rows), 0)
    owner8 = iota((devices * META, rows), 0) >> 3
    field = iota((META, rows), 0)
    place = iota((LANES, rows), 0)
    base = jnp.zeros((devices, 1), f32)
    packed = jnp.zeros((devices * META, LANES), f32)
    for s in range(segs):
        tile = jnp.where(kept, tile_ref[s], -1)
        hot = (tile == owner).astype(f32)
        prefix = jnp.dot(hot.astype(bf16), before, preferred_element_type=f32)
        rank = jnp.sum(hot * (prefix + base), axis=0, keepdims=True).astype(i32)
        base = base + jnp.sum(hot, axis=1, keepdims=True)
        dest = jnp.where(kept, tile * capacity + rank, devices * capacity)
        for h in range(rows // LANES):
            dest_ref[s * (rows // LANES) + h] = dest[:, h * LANES : (h + 1) * LANES]
        offset = off_ref[s : s + 1, :]
        part = rank >> 7
        value = jnp.where(field == part, (offset >> 6) + 1, 0)
        value = jnp.where(field == part + parts, offset & 63, value).astype(f32)
        spread = jnp.concatenate([value] * devices, axis=0)
        stack = jnp.where(tile == owner8, spread, 0.0).astype(bf16)
        spot = (place == (rank & (LANES - 1))).astype(bf16)
        packed = packed + dot_last(stack, spot)
    var = var_ref[...]
    first = var.astype(bf16).astype(f32)
    second = (var - first).astype(bf16).astype(f32)
    third = var - first - second
    row = iota((devices * META, LANES), 0) & (META - 1)
    packed = jnp.where(row == 4, first, packed)
    packed = jnp.where(row == 5, second, packed)
    packed = jnp.where(row == 6, third, packed)
    meta_ref[...] = packed.astype(bf16)


def pack_kernel(raw_ref, above_ref, below_ref, tv_ref, th_ref, dest_ref, meta_ref, out0_ref, out1_ref, edged, vert, conv, spread, sems, *tables):
    rows, cols = raw_ref.shape
    copies = [
        pltpu.make_async_copy(above_ref, edged.at[pl.ds(0, EDGE)], sems.at[0]),
        pltpu.make_async_copy(raw_ref, edged.at[pl.ds(EDGE, rows)], sems.at[1]),
        pltpu.make_async_copy(below_ref, edged.at[pl.ds(EDGE + rows, EDGE)], sems.at[2]),
    ]
    for k, table in enumerate(tables):
        copies.append(pltpu.make_async_copy(dest_ref.at[pl.ds(k, 1)], table, sems.at[3 + k]))
    for copy in copies:
        copy.start()
    vert[:, :LANES] = jnp.zeros((rows, LANES), bf16)
    vert[:, LANES + cols :] = jnp.zeros((rows, LANES), bf16)
    devices, extended, _ = out0_ref.shape
    capacity0 = extended - META
    capacity1 = out1_ref.shape[1]
    out0_ref[:, capacity0:, :] = meta_ref[...].reshape(devices, META, LANES)
    for copy in copies:
        copy.wait()
    wide = 2 * LANES
    tall = rows + 2 * EDGE
    for c in range(cols // wide):
        part = jnp.dot(tv_ref[:, :tall], edged[:, c * wide : (c + 1) * wide], preferred_element_type=f32)
        vert[:, LANES + c * wide : LANES + (c + 1) * wide] = part.astype(bf16)
    for c in range(cols // wide):
        part = dot_last(vert[:, c * wide : c * wide + 2 * wide], th_ref[...])
        conv[2 * c * rows : (2 * c + 1) * rows, :] = part[:, :LANES]
        conv[(2 * c + 1) * rows : (2 * c + 2) * rows, :] = part[:, LANES:]

    def scatter(r, carry):
        for k, table in enumerate(tables):
            spread[pl.ds(table[0, 0, r], 1), :] = conv[pl.ds(r + k * LANES, 1), :]
        return carry

    lax.fori_loop(0, LANES, scatter, 0, unroll=2)

    capacity = capacity0 + capacity1

    def emit(step, carry):
        start = pl.multiple_of(step * capacity, capacity)
        out0_ref[step, :capacity0, :] = spread[pl.ds(start, capacity0), :].astype(bf16)
        out1_ref[step] = spread[pl.ds(start + capacity0, capacity1), :].astype(bf16)
        return carry

    lax.fori_loop(0, devices, emit, 0)


def clear_all(sums, slots):
    def clear(step, carry):
        block = pl.ds(pl.multiple_of(step * 64, 64), 64)
        for acc in sums:
            acc[block, :] = jnp.zeros((64, LANES), f32)
        return carry

    lax.fori_loop(0, slots // 64, clear, 0)


def merged(values):
    while len(values) > 1:
        values = [a + b for a, b in zip(values[::2], values[1::2])] + values[len(values) // 2 * 2 :]
    return values[0]


def place_copies(spots_ref, tables, sems):
    size = tables[0].shape[0]
    return [pltpu.make_async_copy(spots_ref.at[pl.ds(k * size, size)], table, sems.at[k]) for k, table in enumerate(tables)]


def add_rows(tables, scaled, sums, devices, first, count):
    turns = devices // GROUP
    for part in range(tables[0].shape[0] // turns):
        low, high = max(first, part * LANES), min(first + count, (part + 1) * LANES)

        def rank(r, carry):
            for turn in range(turns):
                spots = [table[part * turns + turn, 0, r] for table in tables]
                for half in range(0, GROUP, len(sums)):
                    some = range(half, half + len(sums))
                    held = [acc[pl.ds(spots[k], 1), :] for acc, k in zip(sums, some)]
                    base = part * LANES - first
                    fresh = [scaled[pl.ds(r + (base + (turn * GROUP + k) * count), 1), :] for k in some]
                    for acc, k, one, two in zip(sums, some, held, fresh):
                        acc[pl.ds(spots[k], 1), :] = one + two
            return carry

        if high > low:
            lax.fori_loop(low - part * LANES, high - part * LANES, rank, 0)


def first_kernel(slots, values_ref, spots_out, factor_ref, weight_ref, total_ref, fields, scaled, sems, *rest):
    tables, sums = rest[:GROUP], rest[GROUP:]
    devices, extended, _ = values_ref.shape
    count = extended - META
    parts = spots_out.shape[0] // devices
    fields[...] = values_ref[:, count:, :].astype(f32).reshape(devices * META, LANES)

    def field(k, start=0, step=1):
        return fields[pl.ds(start * META + k, devices // step, stride=step * META), :]

    turns = devices // GROUP
    for g in range(GROUP):
        for k in range(parts):
            high = field(k, g, GROUP)
            spot = jnp.where(high > 0.5, (high - 1.0) * 64.0 + field(parts + k, g, GROUP), float(slots)).astype(i32)
            for t in range(turns):
                spots_out[(g * parts + k) * turns + t] = spot[t : t + 1, :]
    copies = place_copies(spots_out, tables, sems)
    for copy in copies:
        copy.start()
    factor_ref[...] = field(4) + field(5) + field(6)

    clear_all(sums, slots)
    high_id = iota((slots // LANES, LANES), 0)
    low_id = iota((LANES, LANES), 0)

    def weigh(src, weight):
        factor = factor_ref[pl.ds(src, 1), :]
        scaled[pl.ds(pl.multiple_of(src * count, 8), count), :] = values_ref[src, :count, :].astype(f32) * factor
        for k in range(parts):
            spot = spots_out[(src % GROUP * parts + k) * turns + src // GROUP]
            high = ((spot >> 7) == high_id).astype(bf16)
            low = ((spot & (LANES - 1)) == low_id).astype(bf16)
            weight = weight + factor * dot_last(high, low)
        return weight

    weight_ref[...] = lax.fori_loop(0, devices, weigh, jnp.zeros((slots // LANES, LANES), f32))
    for copy in copies:
        copy.wait()
    add_rows(tables, scaled, sums, devices, 0, count)

    def merge(step, carry):
        block = pl.ds(pl.multiple_of(step * 64, 64), 64)
        total_ref[block, :] = merged([acc[block, :] for acc in sums])
        return carry

    lax.fori_loop(0, slots // 64, merge, 0)


def last_kernel(first, values_ref, spots_in, factor_ref, weight_ref, total_ref, image_ref, scaled, sems, *rest):
    tables, sums = rest[:GROUP], rest[GROUP:]
    devices, count, _ = values_ref.shape
    slots = weight_ref.shape[0] * LANES
    copies = place_copies(spots_in, tables, sems)
    copies.append(pltpu.make_async_copy(total_ref, sums[0].at[pl.ds(0, slots)], sems.at[GROUP]))
    for copy in copies:
        copy.start()
    clear_all(sums[1:], slots)

    def weigh(src, carry):
        factor = factor_ref[pl.ds(src, 1), :]
        scaled[pl.ds(pl.multiple_of(src * count, 8), count), :] = values_ref[src].astype(f32) * factor
        return carry

    lax.fori_loop(0, devices, weigh, 0)
    for copy in copies:
        copy.wait()
    add_rows(tables, scaled, sums, devices, first, count)
    for h in range(weight_ref.shape[0]):
        block = slice(h * LANES, (h + 1) * LANES)
        scale = jnp.broadcast_to(jnp.maximum(weight_ref[h : h + 1, :], 1.0), (LANES, LANES)).T
        image_ref[block, :] = merged([acc[block, :] for acc in sums]) / scale


def body(raw_pixels, kernel_bank, kernel_ids, inv_var, gap_start, warp_tile, warp_offset):
    _, rows, cols = raw_pixels.shape
    segs = cols // LANES
    axes = ("expo", "fp")
    devices = lax.axis_size("expo") * lax.axis_size("fp")
    pieces = rows * segs
    capacity = 2 * pieces // devices
    capacity1 = capacity // 4
    capacity0 = capacity - capacity1
    parts = -(-capacity // LANES)
    slots = pieces
    shape = jax.ShapeDtypeStruct

    raw = raw_pixels[0]
    above, below = halo(raw, "fp")
    tiles = jnp.transpose(warp_tile[0], (1, 2, 0))
    offsets = jnp.transpose(warp_offset[0], (1, 0))
    tall = -(-(rows + 2 * EDGE) // LANES) * LANES
    dest, meta, tv, th = pl.pallas_call(
        functools.partial(route_kernel, capacity),
        out_shape=(
            pltpu.VMEM((pieces // LANES, 1, LANES), i32),
            pltpu.VMEM((devices * META, LANES), bf16),
            pltpu.VMEM((rows, tall), bf16),
            pltpu.VMEM((2 * LANES, 4 * LANES), bf16),
        ),
        in_specs=[VMEM] * 6,
        out_specs=(VMEM,) * 4,
        scratch_shapes=[pltpu.VMEM((2, 4 * LANES), f32)],
        cost_estimate=cost(400_000_000, 600_000),
        compiler_params=params(16),
        name="route",
    )(far(tiles), far(offsets), gap_start, inv_var, kernel_ids, far(kernel_bank))

    send0, send1 = pl.pallas_call(
        pack_kernel,
        out_shape=(
            pltpu.VMEM((devices, capacity0 + META, LANES), bf16),
            pltpu.VMEM((devices, capacity1, LANES), bf16),
        ),
        in_specs=[ANY, ANY, ANY, VMEM, VMEM, VMEM, VMEM],
        out_specs=(VMEM, VMEM),
        scratch_shapes=[
            pltpu.VMEM((rows + 2 * EDGE, cols), bf16),
            pltpu.VMEM((rows, cols + 2 * LANES), bf16),
            pltpu.VMEM((pieces, LANES), f32),
            pltpu.VMEM((devices * capacity + 8, LANES), f32),
            pltpu.SemaphoreType.DMA((3 + pieces // LANES,)),
        ]
        + [pltpu.SMEM((1, 1, LANES), i32)] * (pieces // LANES),
        cost_estimate=cost(10_000_000_000, 4_000_000),
        compiler_params=params(24),
        name="pack",
    )(far(raw), near(above), near(below), near(tv), near(th), near(dest), near(meta))

    got0 = lax.all_to_all(send0, axes, split_axis=0, concat_axis=0, tiled=True)
    got1 = lax.all_to_all(send1, axes, split_axis=0, concat_axis=0, tiled=True)

    tables = [pltpu.SemaphoreType.DMA((GROUP + 1,))] + [pltpu.SMEM((parts * devices // GROUP, 1, LANES), i32)] * GROUP
    spots, factor, weight, total = pl.pallas_call(
        functools.partial(first_kernel, slots),
        out_shape=(
            pltpu.VMEM((parts * devices, 1, LANES), i32),
            pltpu.VMEM((devices, LANES), f32),
            pltpu.VMEM((slots // LANES, LANES), f32),
            pltpu.HBM((slots, LANES), f32),
        ),
        in_specs=[VMEM],
        out_specs=(VMEM,) * 4,
        scratch_shapes=[
            pltpu.VMEM((devices * META, LANES), f32),
            pltpu.VMEM((devices * capacity0, LANES), f32),
            *tables,
        ]
        + [pltpu.VMEM((slots + 8, LANES), f32)] * SPLIT[0],
        cost_estimate=cost(10_000_000_000, 4_000_000),
        compiler_params=params(28),
        name="sum_first",
    )(near(got0))
    image = pl.pallas_call(
        functools.partial(last_kernel, capacity0),
        out_shape=shape((slots, LANES), f32),
        in_specs=[VMEM] * 4 + [ANY],
        out_specs=VMEM,
        scratch_shapes=[pltpu.VMEM((devices * capacity1, LANES), f32), *tables]
        + [pltpu.VMEM((slots + 8, LANES), f32)] * SPLIT[1],
        cost_estimate=cost(10_000_000_000, 4_000_000),
        compiler_params=params(20),
        name="sum_last",
    )(near(got1), near(spots), near(factor), near(weight), far(total))
    return image[None], weight.reshape(1, slots)


def solution(mesh):
    in_specs = (
        P("expo", "fp", None),
        P(),
        P("expo", "fp"),
        P("expo", "fp"),
        P("expo", "fp"),
        P("expo", "fp", None, None),
        P("expo", "fp", None),
    )
    out_specs = (P(("expo", "fp"), None, None), P(("expo", "fp"), None))
    return jax.shard_map(body, mesh=mesh, in_specs=in_specs, out_specs=out_specs, check_vma=False)
```

```python
import functools

import jax
import jax.numpy as jnp
from jax import lax
from jax.experimental import pallas as pl
from jax.experimental.pallas import tpu as pltpu
from jax.sharding import PartitionSpec as P

GAP = 32
EDGE = 32
LANES = 128
META = 8
GROUP = 8
TAIL = 2


VMEM = pl.BlockSpec(memory_space=pltpu.VMEM)
ANY = pl.BlockSpec(memory_space=pl.ANY)
f32, bf16, i32 = jnp.float32, jnp.bfloat16, jnp.int32


def iota(shape, dim):
    return lax.broadcasted_iota(i32, shape, dim)


def dot_last(a, b):
    return lax.dot_general(a, b, (((1,), (1,)), ((), ())), preferred_element_type=f32)


def near(x):
    return pltpu.with_memory_space_constraint(x, pltpu.VMEM)


def far(x):
    return pltpu.with_memory_space_constraint(x, pltpu.HBM)


def params(mib):
    return pltpu.CompilerParams(vmem_limit_bytes=mib << 20)


def cost(flops, moved):
    return pl.CostEstimate(flops=flops, bytes_accessed=moved, transcendentals=0)


def halo(shard, axis):
    size = lax.axis_size(axis)
    up = [(i, i + 1) for i in range(size - 1)]
    down = [(i + 1, i) for i in range(size - 1)]
    above = lax.ppermute(shard[-EDGE:], axis, up)
    below = lax.ppermute(shard[:EDGE], axis, down)
    return above, below


def route_kernel(capacity, tile_ref, off_ref, own_ref, bank_ref, dest_ref, meta_ref, tv_ref, th_ref, line_ref):
    segs, rows = off_ref.shape
    devices = meta_ref.shape[0] // META
    parts = -(-capacity // LANES)
    own = own_ref[...]
    gap, var, which_bank, me = [own[k : k + 1, :1] for k in range(4)]
    gap, which_bank, me = gap.astype(i32), which_bank.astype(i32), me.astype(i32)
    bank = bank_ref[...].astype(f32)
    chosen = jnp.where(which_bank == 0, bank[0], 0.0)
    for k in range(1, bank.shape[0]):
        chosen = jnp.where(which_bank == k, bank[k], chosen)
    taps = bank.shape[2]
    half = taps // 2
    lead = -half % 8
    line_ref[...] = jnp.zeros(line_ref.shape, f32)
    line_ref[:, lead : lead + taps] = chosen
    for ref, which, shift in ((tv_ref, 0, EDGE - half), (th_ref, 1, LANES - half)):
        height, width = ref.shape
        wide = jnp.broadcast_to(line_ref[which : which + 1, :width], (height, width))
        ref[...] = pltpu.roll(wide, shift - lead, 1, stride=1, stride_axis=0).astype(bf16)
    line = iota((1, rows), 1)
    kept = jnp.logical_or(line < gap, line >= gap + GAP)
    before = (iota((rows, rows), 0) < iota((rows, rows), 1)).astype(bf16)
    owner = iota((devices, rows), 0)
    owner8 = iota((devices * META, rows), 0) >> 3
    field = iota((META, rows), 0)
    place = iota((LANES, rows), 0)
    base = jnp.zeros((devices, 1), f32)
    packed = jnp.zeros((devices * META, LANES), f32)
    for s in range(segs):
        tile = tile_ref[s] - me
        tile = jnp.where(tile < 0, tile + devices, tile)
        tile = jnp.where(kept, tile, -1)
        hot = (tile == owner).astype(f32)
        prefix = jnp.dot(hot.astype(bf16), before, preferred_element_type=f32)
        rank = jnp.sum(hot * (prefix + base), axis=0, keepdims=True).astype(i32)
        base = base + jnp.sum(hot, axis=1, keepdims=True)
        dest = jnp.where(kept, tile * capacity + rank, devices * capacity)
        for h in range(rows // LANES):
            dest_ref[s * (rows // LANES) + h] = dest[:, h * LANES : (h + 1) * LANES]
        offset = off_ref[s : s + 1, :]
        part = rank >> 7
        value = jnp.where(field == part, (offset >> 6) + 1, 0)
        value = jnp.where(field == part + parts, offset & 63, value).astype(f32)
        spread = jnp.concatenate([value] * devices, axis=0)
        stack = jnp.where(tile == owner8, spread, 0.0).astype(bf16)
        spot = (place == (rank & (LANES - 1))).astype(bf16)
        packed = packed + dot_last(stack, spot)
    first = var.astype(bf16).astype(f32)
    second = (var - first).astype(bf16).astype(f32)
    third = var - first - second
    row = iota((devices * META, LANES), 0) & (META - 1)
    packed = jnp.where(row == 4, first, packed)
    packed = jnp.where(row == 5, second, packed)
    packed = jnp.where(row == 6, third, packed)
    meta_ref[...] = packed.astype(bf16)


def pack_kernel(devices, raw_ref, above_ref, below_ref, tv_ref, th_ref, dest_ref, meta_ref, *rest):
    outs, (edged, vert, conv, spread, sems, *tables) = rest[:devices], rest[devices:]
    rows, cols = raw_ref.shape
    copies = [
        pltpu.make_async_copy(above_ref, edged.at[pl.ds(0, EDGE)], sems.at[0]),
        pltpu.make_async_copy(raw_ref, edged.at[pl.ds(EDGE, rows)], sems.at[1]),
        pltpu.make_async_copy(below_ref, edged.at[pl.ds(EDGE + rows, EDGE)], sems.at[2]),
    ]
    for k, table in enumerate(tables):
        copies.append(pltpu.make_async_copy(dest_ref.at[pl.ds(k, 1)], table, sems.at[3 + k]))
    for copy in copies:
        copy.start()
    vert[:, :LANES] = jnp.zeros((rows, LANES), bf16)
    vert[:, LANES + cols :] = jnp.zeros((rows, LANES), bf16)
    capacity = outs[0].shape[0] - META
    for k, out in enumerate(outs):
        out[capacity:, :] = meta_ref[k * META : (k + 1) * META, :]
    for copy in copies:
        copy.wait()
    wide = 2 * LANES
    tall = rows + 2 * EDGE
    for c in range(cols // wide):
        part = jnp.dot(tv_ref[:, :tall], edged[:, c * wide : (c + 1) * wide], preferred_element_type=f32)
        vert[:, LANES + c * wide : LANES + (c + 1) * wide] = part.astype(bf16)
    for c in range(cols // wide):
        part = dot_last(vert[:, c * wide : c * wide + 2 * wide], th_ref[...])
        conv[2 * c * rows : (2 * c + 1) * rows, :] = part[:, :LANES]
        conv[(2 * c + 1) * rows : (2 * c + 2) * rows, :] = part[:, LANES:]

    def scatter(r, carry):
        for k, table in enumerate(tables):
            spread[pl.ds(table[0, 0, r], 1), :] = conv[pl.ds(r + k * LANES, 1), :]
        return carry

    lax.fori_loop(0, LANES, scatter, 0, unroll=2)
    for k, out in enumerate(outs):
        out[:capacity, :] = spread[k * capacity : (k + 1) * capacity, :].astype(bf16)


def sum_kernel(slots, opens, closes, count, *refs):
    values, refs = refs[:count], refs[count:]
    if not opens:
        (total_in, weight_in), refs = refs[:2], refs[2:]
    (total_out, weight_out), refs = refs[:2], refs[2:]
    (scaled, spots, sems), refs = refs[:3], refs[3:]
    tables, sums = refs[:count], refs[count:]
    capacity = values[0].shape[0] - META
    parts = -(-capacity // LANES)
    lanes = min(capacity, LANES)
    copies = []
    if not opens:
        copies.append(pltpu.make_async_copy(total_in, sums[0].at[pl.ds(8, slots)], sems.at[count]))
        copies[-1].start()
    high_id = iota((slots // LANES, LANES), 0)
    low_id = iota((LANES, LANES), 0)
    weight = jnp.zeros((slots // LANES, LANES), f32) if opens else weight_in[...]
    for k in range(count):
        fields = values[k][capacity:, :].astype(f32)
        factor = fields[4:5, :] + fields[5:6, :] + fields[6:7, :]
        for p in range(parts):
            high, low = fields[p : p + 1, :], fields[parts + p : parts + p + 1, :]
            slot = jnp.where(high > 0.5, (high - 1.0) * 64.0 + low, float(slots)).astype(i32)
            spots[k * parts + p] = slot + (8 - k)
            high = ((slot >> 7) == high_id).astype(bf16)
            low = ((slot & (LANES - 1)) == low_id).astype(bf16)
            weight = weight + factor * dot_last(high, low)
        copies.append(pltpu.make_async_copy(spots.at[pl.ds(k * parts, parts)], tables[k], sems.at[k]))
        copies[-1].start()
        scaled[pl.ds(k, capacity, stride=GROUP), :] = values[k][:capacity, :].astype(f32) * factor
    weight_out[...] = weight

    def clear(step, carry):
        block = pl.ds(pl.multiple_of(step * 64 + 8, 8), 64)
        for acc in sums if opens else sums[1:]:
            acc[block, :] = jnp.zeros((64, LANES), f32)
        return carry

    lax.fori_loop(0, slots // 64, clear, 0)
    for copy in copies:
        copy.wait()
    member = iota((GROUP, LANES), 0)
    for p in range(parts):

        def rank(r, carry):
            places = [table[p, 0, r] for table in tables]
            start = (r + p * LANES) * GROUP
            fresh = scaled[pl.ds(pl.multiple_of(start, GROUP), GROUP), :]
            held = [acc[pl.ds(place, GROUP), :] for acc, place in zip(sums, places)]
            for k in range(count):
                sums[k][pl.ds(places[k], GROUP), :] = held[k] + jnp.where(member == k, fresh, 0.0)
            return carry

        lax.fori_loop(0, lanes, rank, 0, unroll=4)

    for h in range(slots // LANES):
        block = slice(h * LANES, (h + 1) * LANES)
        total = [acc[8 + h * LANES : 8 + (h + 1) * LANES, :] for acc in sums]
        while len(total) > 1:
            total = [a + b for a, b in zip(total[::2], total[1::2])] + total[len(total) // 2 * 2 :]
        if closes:
            scale = jnp.broadcast_to(jnp.maximum(weight[h : h + 1, :], 1.0), (LANES, LANES)).T
            total_out[block, :] = total[0] / scale
        else:
            total_out[block, :] = total[0]


def body(raw_pixels, kernel_bank, kernel_ids, inv_var, gap_start, warp_tile, warp_offset):
    _, rows, cols = raw_pixels.shape
    segs = cols // LANES
    axes = ("expo", "fp")
    devices = lax.axis_size("expo") * lax.axis_size("fp")
    pieces = rows * segs
    capacity = 2 * pieces // devices
    parts = -(-capacity // LANES)
    slots = pieces
    shape = jax.ShapeDtypeStruct

    raw = raw_pixels[0]
    above, below = halo(raw, "fp")
    tiles = jnp.transpose(warp_tile[0], (1, 2, 0))
    offsets = jnp.transpose(warp_offset[0], (1, 0))
    tall = -(-(rows + 2 * EDGE) // LANES) * LANES
    row = iota((8, LANES), 0)
    own = jnp.where(row == 0, gap_start.astype(f32), inv_var)
    own = jnp.where(row == 2, kernel_ids.astype(f32), own)
    own = jnp.where(row == 3, lax.axis_index(axes).astype(f32), own)
    dest, meta, tv, th = pl.pallas_call(
        functools.partial(route_kernel, capacity),
        out_shape=(
            pltpu.VMEM((pieces // LANES, 1, LANES), i32),
            pltpu.VMEM((devices * META, LANES), bf16),
            pltpu.VMEM((rows, tall), bf16),
            pltpu.VMEM((2 * LANES, 4 * LANES), bf16),
        ),
        in_specs=[VMEM] * 4,
        out_specs=(VMEM,) * 4,
        scratch_shapes=[pltpu.VMEM((2, 4 * LANES), f32)],
        cost_estimate=cost(400_000_000, 600_000),
        compiler_params=params(16),
        name="route",
    )(far(tiles), far(offsets), near(own), far(kernel_bank))

    sends = pl.pallas_call(
        functools.partial(pack_kernel, devices),
        out_shape=(pltpu.VMEM((capacity + META, LANES), bf16),) * devices,
        in_specs=[ANY, ANY, ANY, VMEM, VMEM, VMEM, VMEM],
        out_specs=(VMEM,) * devices,
        scratch_shapes=[
            pltpu.VMEM((rows + 2 * EDGE, cols), bf16),
            pltpu.VMEM((rows, cols + 2 * LANES), bf16),
            pltpu.VMEM((pieces, LANES), f32),
            pltpu.VMEM((devices * capacity + 8, LANES), f32),
            pltpu.SemaphoreType.DMA((3 + pieces // LANES,)),
        ]
        + [pltpu.SMEM((1, 1, LANES), i32)] * (pieces // LANES),
        cost_estimate=cost(10_000_000_000, 4_000_000),
        compiler_params=params(20),
        name="pack",
    )(far(raw), near(above), near(below), near(tv), near(th), near(dest), near(meta))

    got = [sends[0]]
    for k in range(1, devices):
        got.append(lax.ppermute(sends[k], axes, [(i, (i + k) % devices) for i in range(devices)]))

    cuts = [*range(0, devices - GROUP + 1, GROUP), devices - TAIL, devices]
    state = []
    for low, high in zip(cuts, cuts[1:]):
        count = high - low
        opens, closes = low == 0, high == devices
        state = pl.pallas_call(
            functools.partial(sum_kernel, slots, opens, closes, count),
            out_shape=(shape((slots, LANES), f32) if closes else pltpu.HBM((slots, LANES), f32), shape((slots // LANES, LANES), f32)),
            in_specs=[VMEM] * count + ([] if opens else [ANY, VMEM]),
            out_specs=(VMEM, VMEM),
            scratch_shapes=[
                pltpu.VMEM((capacity * GROUP, LANES), f32),
                pltpu.VMEM((GROUP * parts, 1, LANES), i32),
                pltpu.SemaphoreType.DMA((GROUP + 1,)),
            ]
            + [pltpu.SMEM((parts, 1, LANES), i32)] * count
            + [pltpu.VMEM((slots + 24, LANES), f32)] * count,
            cost_estimate=cost(4_000_000_000, 8_000_000),
            compiler_params=params(26),
            name=f"sum_{low}",
        )(*[near(x) for x in got[low:high]], *([] if opens else [far(state[0]), state[1]]))
    image, weight = state
    return image[None], weight.reshape(1, slots)


def solution(mesh):
    in_specs = (
        P("expo", "fp", None),
        P(),
        P("expo", "fp"),
        P("expo", "fp"),
        P("expo", "fp"),
        P("expo", "fp", None, None),
        P("expo", "fp", None),
    )
    out_specs = (P(("expo", "fp"), None, None), P(("expo", "fp"), None))
    return jax.shard_map(body, mesh=mesh, in_specs=in_specs, out_specs=out_specs, check_vma=False)
```

```python
import functools

import jax
import jax.numpy as jnp
from jax import lax
from jax.experimental import pallas as pl
from jax.experimental.pallas import tpu as pltpu
from jax.sharding import PartitionSpec as P

GAP = 32
EDGE = 32
LANES = 128
META = 8
GROUP = 8
SPLIT = 8


VMEM = pl.BlockSpec(memory_space=pltpu.VMEM)
ANY = pl.BlockSpec(memory_space=pl.ANY)
f32, bf16, i32 = jnp.float32, jnp.bfloat16, jnp.int32


def iota(shape, dim):
    return lax.broadcasted_iota(i32, shape, dim)


def dot_last(a, b):
    return lax.dot_general(a, b, (((1,), (1,)), ((), ())), preferred_element_type=f32)


def near(x):
    return pltpu.with_memory_space_constraint(x, pltpu.VMEM)


def far(x):
    return pltpu.with_memory_space_constraint(x, pltpu.HBM)


def params(mib):
    return pltpu.CompilerParams(vmem_limit_bytes=mib << 20)


def cost(flops, moved):
    return pl.CostEstimate(flops=flops, bytes_accessed=moved, transcendentals=0)


def halo(shard, axis):
    size = lax.axis_size(axis)
    up = [(i, i + 1) for i in range(size - 1)]
    down = [(i + 1, i) for i in range(size - 1)]
    above = lax.ppermute(shard[-EDGE:], axis, up)
    below = lax.ppermute(shard[:EDGE], axis, down)
    return above, below


def route_kernel(capacity, tile_ref, off_ref, gap_ref, var_ref, id_ref, bank_ref, dest_ref, meta_ref, tv_ref, th_ref, line_ref):
    segs, rows = off_ref.shape
    devices = meta_ref.shape[0] // META
    parts = -(-capacity // LANES)
    gap, var, which_bank = gap_ref[...], var_ref[...], id_ref[...]
    bank = bank_ref[...].astype(f32)
    chosen = jnp.where(which_bank == 0, bank[0], 0.0)
    for k in range(1, bank.shape[0]):
        chosen = jnp.where(which_bank == k, bank[k], chosen)
    taps = bank.shape[2]
    half = taps // 2
    lead = -half % 8
    line_ref[...] = jnp.zeros(line_ref.shape, f32)
    line_ref[:, lead : lead + taps] = chosen
    for ref, which, shift in ((tv_ref, 0, EDGE - half), (th_ref, 1, LANES - half)):
        height, width = ref.shape
        wide = jnp.broadcast_to(line_ref[which : which + 1, :width], (height, width))
        ref[...] = pltpu.roll(wide, shift - lead, 1, stride=1, stride_axis=0).astype(bf16)
    line = iota((1, rows), 1)
    kept = jnp.logical_or(line < gap, line >= gap + GAP)
    before = (iota((rows, rows), 0) < iota((rows, rows), 1)).astype(bf16)
    owner = iota((devices, rows), 0)
    owner8 = iota((devices * META, rows), 0) >> 3
    field = iota((META, rows), 0)
    place = iota((LANES, rows), 0)
    base = jnp.zeros((devices, 1), f32)
    packed = jnp.zeros((devices * META, LANES), f32)
    for s in range(segs):
        tile = jnp.where(kept, tile_ref[s], -1)
        hot = (tile == owner).astype(f32)
        prefix = jnp.dot(hot.astype(bf16), before, preferred_element_type=f32)
        rank = jnp.sum(hot * (prefix + base), axis=0, keepdims=True).astype(i32)
        base = base + jnp.sum(hot, axis=1, keepdims=True)
        dest = jnp.where(kept, tile * capacity + rank, devices * capacity)
        for h in range(rows // LANES):
            dest_ref[s * (rows // LANES) + h] = dest[:, h * LANES : (h + 1) * LANES]
        offset = off_ref[s : s + 1, :]
        part = rank >> 7
        value = jnp.where(field == part, (offset >> 6) + 1, 0)
        value = jnp.where(field == part + parts, offset & 63, value).astype(f32)
        spread = jnp.concatenate([value] * devices, axis=0)
        stack = jnp.where(tile == owner8, spread, 0.0).astype(bf16)
        spot = (place == (rank & (LANES - 1))).astype(bf16)
        packed = packed + dot_last(stack, spot)
    first = var.astype(bf16).astype(f32)
    second = (var - first).astype(bf16).astype(f32)
    third = var - first - second
    row = iota((devices * META, LANES), 0) & (META - 1)
    packed = jnp.where(row == 4, first, packed)
    packed = jnp.where(row == 5, second, packed)
    packed = jnp.where(row == 6, third, packed)
    meta_ref[...] = packed.astype(bf16)


def own_index():
    return lax.axis_index("expo") * lax.axis_size("fp") + lax.axis_index("fp")


def pack_kernel(near_peers, raw_ref, above_ref, below_ref, tv_ref, th_ref, dest_ref, meta_ref, all_ref, *rest):
    outs, (edged, vert, conv, spread, stage, sems, *tables) = rest[: len(near_peers)], rest[len(near_peers) :]
    me = own_index()
    devices, extended, _ = all_ref.shape
    capacity = extended - META
    rows, cols = raw_ref.shape
    copies = [
        pltpu.make_async_copy(above_ref, edged.at[pl.ds(0, EDGE)], sems.at[0]),
        pltpu.make_async_copy(raw_ref, edged.at[pl.ds(EDGE, rows)], sems.at[1]),
        pltpu.make_async_copy(below_ref, edged.at[pl.ds(EDGE + rows, EDGE)], sems.at[2]),
    ]
    for k, table in enumerate(tables):
        copies.append(pltpu.make_async_copy(dest_ref.at[pl.ds(k, 1)], table, sems.at[3 + k]))
    for copy in copies:
        copy.start()
    vert[:, :LANES] = jnp.zeros((rows, LANES), bf16)
    vert[:, LANES + cols :] = jnp.zeros((rows, LANES), bf16)
    stage[:, capacity:, :] = meta_ref[...].reshape(devices, META, LANES)
    for k, out in zip(near_peers, outs):
        out[capacity:, :] = meta_ref[pl.ds(pl.multiple_of((me ^ k) * META, META), META), :]
    for copy in copies:
        copy.wait()
    wide = 2 * LANES
    tall = rows + 2 * EDGE
    for c in range(cols // wide):
        part = jnp.dot(tv_ref[:, :tall], edged[:, c * wide : (c + 1) * wide], preferred_element_type=f32)
        vert[:, LANES + c * wide : LANES + (c + 1) * wide] = part.astype(bf16)
    for c in range(cols // wide):
        part = dot_last(vert[:, c * wide : c * wide + 2 * wide], th_ref[...])
        conv[2 * c * rows : (2 * c + 1) * rows, :] = part[:, :LANES]
        conv[(2 * c + 1) * rows : (2 * c + 2) * rows, :] = part[:, LANES:]

    def scatter(r, carry):
        for k, table in enumerate(tables):
            spread[pl.ds(table[0, 0, r], 1), :] = conv[pl.ds(r + k * LANES, 1), :]
        return carry

    lax.fori_loop(0, LANES, scatter, 0, unroll=2)

    def emit(k, carry):
        stage[k, :capacity, :] = spread[pl.ds(pl.multiple_of(k * capacity, 8), capacity), :].astype(bf16)
        return carry

    share = devices // 4
    copies = []
    for g in range(4):
        lax.fori_loop(g * share, (g + 1) * share, emit, 0)
        block = pl.ds(g * share, share)
        copies.append(pltpu.make_async_copy(stage.at[block], all_ref.at[block], sems.at[g]))
        copies[-1].start()
    for k, out in zip(near_peers, outs):
        out[:capacity, :] = spread[pl.ds(pl.multiple_of((me ^ k) * capacity, 8), capacity), :].astype(bf16)
    for copy in copies:
        copy.wait()


def sum_kernel(slots, peers, closes, *refs):
    if closes:
        (values, total_in, weight_in), refs = refs[:3], refs[3:]
        me = own_index()
        sources = [values.at[me ^ k] for k in peers]
    else:
        sources, refs = refs[: len(peers)], refs[len(peers) :]
    (total_out, weight_out, scaled, spots, stage, sems), refs = refs[:6], refs[6:]
    sums, tables = refs[:SPLIT], refs[SPLIT:]
    capacity = sources[0].shape[0] - META
    parts = -(-capacity // LANES)
    lanes = min(capacity, LANES)
    turns = len(peers) // GROUP
    copies = []
    if closes:
        copies.append(pltpu.make_async_copy(total_in, sums[0].at[pl.ds(8, slots)], sems.at[len(tables)]))
        copies[0].start()
    high_id = iota((slots // LANES, LANES), 0)
    low_id = iota((LANES, LANES), 0)
    weight = weight_in[...] if closes else jnp.zeros((slots // LANES, LANES), f32)
    for n, source in enumerate(sources):
        turn, member = divmod(n, GROUP)
        fields = source[capacity:, :].astype(f32)
        factor = fields[4:5, :] + fields[5:6, :] + fields[6:7, :]
        for p in range(parts):
            high, low = fields[p : p + 1, :], fields[parts + p : parts + p + 1, :]
            slot = jnp.where(high > 0.5, (high - 1.0) * 64.0 + low, float(slots)).astype(i32)
            spots[n * parts + p] = slot + (8 - member)
            high = ((slot >> 7) == high_id).astype(bf16)
            low = ((slot & (LANES - 1)) == low_id).astype(bf16)
            weight = weight + factor * dot_last(high, low)
        scaled[pl.ds(turn * capacity * GROUP + member, capacity, stride=GROUP), :] = source[:capacity, :].astype(f32) * factor
    for k, table in enumerate(tables):
        copies.append(pltpu.make_async_copy(spots.at[pl.ds(k, 1)], table, sems.at[k]))
        copies[-1].start()
    weight_out[...] = weight

    def clear(step, carry):
        block = pl.ds(pl.multiple_of(step * 64 + 8, 8), 64)
        for acc in sums[1:] if closes else sums:
            acc[block, :] = jnp.zeros((64, LANES), f32)
        return carry

    lax.fori_loop(0, slots // 64, clear, 0)
    for copy in copies:
        copy.wait()
    member = iota((GROUP, LANES), 0)
    for p in range(parts):
        for turn in range(turns):

            def rank(r, carry):
                places = [tables[(turn * GROUP + k) * parts + p][0, 0, r] for k in range(GROUP)]
                start = (r + (turn * capacity + p * LANES)) * GROUP
                fresh = scaled[pl.ds(pl.multiple_of(start, GROUP), GROUP), :]
                for first in range(0, GROUP, len(sums)):
                    some = range(first, first + len(sums))
                    held = [acc[pl.ds(places[k], GROUP), :] for acc, k in zip(sums, some)]
                    for acc, k, was in zip(sums, some, held):
                        acc[pl.ds(places[k], GROUP), :] = was + jnp.where(member == k, fresh, 0.0)
                return carry

            lax.fori_loop(0, lanes, rank, 0, unroll=8)

    copies = []
    quarter = slots // LANES // 4
    for h in range(slots // LANES):
        block = slice(h * LANES, (h + 1) * LANES)
        total = [acc[8 + h * LANES : 8 + (h + 1) * LANES, :] for acc in sums]
        while len(total) > 1:
            total = [a + b for a, b in zip(total[::2], total[1::2])] + total[len(total) // 2 * 2 :]
        if closes:
            scale = jnp.broadcast_to(jnp.maximum(weight[h : h + 1, :], 1.0), (LANES, LANES)).T
            stage[block, :] = total[0] / scale
        else:
            stage[block, :] = total[0]
        if h % quarter == quarter - 1:
            ready = pl.ds((h + 1 - quarter) * LANES, quarter * LANES)
            copies.append(pltpu.make_async_copy(stage.at[ready], total_out.at[ready], sems.at[h // quarter]))
            copies[-1].start()
    for copy in copies:
        copy.wait()


def body(raw_pixels, kernel_bank, kernel_ids, inv_var, gap_start, warp_tile, warp_offset):
    _, rows, cols = raw_pixels.shape
    segs = cols // LANES
    axes = ("expo", "fp")
    devices = lax.axis_size("expo") * lax.axis_size("fp")
    pieces = rows * segs
    capacity = 2 * pieces // devices
    parts = -(-capacity // LANES)
    slots = pieces
    shape = jax.ShapeDtypeStruct

    raw = raw_pixels[0]
    above, below = halo(raw, "fp")
    tiles = jnp.transpose(warp_tile[0], (1, 2, 0))
    offsets = jnp.transpose(warp_offset[0], (1, 0))
    tall = -(-(rows + 2 * EDGE) // LANES) * LANES
    dest, meta, tv, th = pl.pallas_call(
        functools.partial(route_kernel, capacity),
        out_shape=(
            pltpu.VMEM((pieces // LANES, 1, LANES), i32),
            pltpu.VMEM((devices * META, LANES), bf16),
            pltpu.VMEM((rows, tall), bf16),
            pltpu.VMEM((2 * LANES, 4 * LANES), bf16),
        ),
        in_specs=[VMEM] * 6,
        out_specs=(VMEM,) * 4,
        scratch_shapes=[pltpu.VMEM((2, 4 * LANES), f32)],
        cost_estimate=cost(400_000_000, 600_000),
        compiler_params=params(16),
        name="route",
    )(far(tiles), far(offsets), gap_start, inv_var, kernel_ids, far(kernel_bank))

    bit = lax.axis_size("fp") // 2
    near_peers = [k for k in range(devices) if not k & bit]
    far_peers = [k for k in range(devices) if k & bit]
    everything, *sends = pl.pallas_call(
        functools.partial(pack_kernel, near_peers),
        out_shape=(pltpu.HBM((devices, capacity + META, LANES), bf16),)
        + (pltpu.VMEM((capacity + META, LANES), bf16),) * len(near_peers),
        in_specs=[ANY, ANY, ANY, VMEM, VMEM, VMEM, VMEM],
        out_specs=(ANY,) + (VMEM,) * len(near_peers),
        scratch_shapes=[
            pltpu.VMEM((rows + 2 * EDGE, cols), bf16),
            pltpu.VMEM((rows, cols + 2 * LANES), bf16),
            pltpu.VMEM((pieces, LANES), f32),
            pltpu.VMEM((devices * capacity + 8, LANES), f32),
            pltpu.VMEM((devices, capacity + META, LANES), bf16),
            pltpu.SemaphoreType.DMA((3 + pieces // LANES,)),
        ]
        + [pltpu.SMEM((1, 1, LANES), i32)] * (pieces // LANES),
        cost_estimate=cost(10_000_000_000, 4_000_000),
        compiler_params=params(20),
        name="pack",
    )(far(raw), near(above), near(below), near(tv), near(th), near(dest), near(meta))

    got = lax.all_to_all(everything, axes, split_axis=0, concat_axis=0, tiled=True)
    some = [sends[0]]
    for k, send in zip(near_peers[1:], sends[1:]):
        some.append(lax.ppermute(send, axes, [(i, i ^ k) for i in range(devices)]))

    def add_up(peers, closes, *args):
        turns = len(peers) // GROUP
        return pl.pallas_call(
            functools.partial(sum_kernel, slots, peers, closes),
            out_shape=(
                pltpu.HBM((slots, LANES), f32),
                shape((slots // LANES, LANES), f32),
            ),
            in_specs=[VMEM, ANY, VMEM] if closes else [VMEM] * len(peers),
            out_specs=(ANY, VMEM),
            scratch_shapes=[
                pltpu.VMEM((capacity * GROUP * turns, LANES), f32),
                pltpu.VMEM((GROUP * turns * parts, 1, LANES), i32),
                pltpu.VMEM((slots, LANES), f32),
                pltpu.SemaphoreType.DMA((len(peers) * parts + 1,)),
            ]
            + [pltpu.VMEM((slots + 24, LANES), f32)] * SPLIT
            + [pltpu.SMEM((1, 1, LANES), i32)] * (len(peers) * parts),
            cost_estimate=cost(4_000_000_000, 8_000_000),
            compiler_params=params(28),
            name="sum_far" if closes else "sum_near",
        )(*args)

    total, weight = add_up(near_peers, False, *[near(x) for x in some])
    image, weight = add_up(far_peers, True, near(got), far(total), weight)
    return image[None], weight.reshape(1, slots)


def solution(mesh):
    in_specs = (
        P("expo", "fp", None),
        P(),
        P("expo", "fp"),
        P("expo", "fp"),
        P("expo", "fp"),
        P("expo", "fp", None, None),
        P("expo", "fp", None),
    )
    out_specs = (P(("expo", "fp"), None, None), P(("expo", "fp"), None))
    return jax.shard_map(body, mesh=mesh, in_specs=in_specs, out_specs=out_specs, check_vma=False)
```

```python
import functools

import jax
import jax.numpy as jnp
from jax import lax
from jax.experimental import pallas as pl
from jax.experimental.pallas import tpu as pltpu
from jax.sharding import PartitionSpec as P

GAP = 32
EDGE = 32
LANES = 128
META = 8
GROUP = 8


VMEM = pl.BlockSpec(memory_space=pltpu.VMEM)
ANY = pl.BlockSpec(memory_space=pl.ANY)
f32, bf16, i32 = jnp.float32, jnp.bfloat16, jnp.int32


def iota(shape, dim):
    return lax.broadcasted_iota(i32, shape, dim)


def dot_last(a, b):
    return lax.dot_general(a, b, (((1,), (1,)), ((), ())), preferred_element_type=f32)


def near(x):
    return pltpu.with_memory_space_constraint(x, pltpu.VMEM)


def far(x):
    return pltpu.with_memory_space_constraint(x, pltpu.HBM)


def params(mib):
    return pltpu.CompilerParams(vmem_limit_bytes=mib << 20)


def cost(flops, moved):
    return pl.CostEstimate(flops=flops, bytes_accessed=moved, transcendentals=0)


def halo(shard, axis):
    size = lax.axis_size(axis)
    up = [(i, i + 1) for i in range(size - 1)]
    down = [(i + 1, i) for i in range(size - 1)]
    above = lax.ppermute(shard[-EDGE:], axis, up)
    below = lax.ppermute(shard[:EDGE], axis, down)
    return above, below


def route_kernel(capacity, tile_ref, off_ref, gap_ref, var_ref, id_ref, bank_ref, dest_ref, meta_ref, tv_ref, th_ref, line_ref):
    segs, rows = off_ref.shape
    devices = meta_ref.shape[0] // META
    parts = -(-capacity // LANES)
    gap, var, which_bank = gap_ref[...], var_ref[...], id_ref[...]
    bank = bank_ref[...].astype(f32)
    chosen = jnp.where(which_bank == 0, bank[0], 0.0)
    for k in range(1, bank.shape[0]):
        chosen = jnp.where(which_bank == k, bank[k], chosen)
    taps = bank.shape[2]
    half = taps // 2
    lead = -half % 8
    line_ref[...] = jnp.zeros(line_ref.shape, f32)
    line_ref[:, lead : lead + taps] = chosen
    for ref, which, shift in ((tv_ref, 0, EDGE - half), (th_ref, 1, LANES - half)):
        height, width = ref.shape
        wide = jnp.broadcast_to(line_ref[which : which + 1, :width], (height, width))
        ref[...] = pltpu.roll(wide, shift - lead, 1, stride=1, stride_axis=0).astype(bf16)
    line = iota((1, rows), 1)
    kept = jnp.logical_or(line < gap, line >= gap + GAP)
    before = (iota((rows, rows), 0) < iota((rows, rows), 1)).astype(bf16)
    owner = iota((devices, rows), 0)
    owner8 = iota((devices * META, rows), 0) >> 3
    field = iota((META, rows), 0)
    place = iota((LANES, rows), 0)
    base = jnp.zeros((devices, 1), f32)
    packed = jnp.zeros((devices * META, LANES), f32)
    for s in range(segs):
        tile = jnp.where(kept, tile_ref[s], -1)
        hot = (tile == owner).astype(f32)
        prefix = jnp.dot(hot.astype(bf16), before, preferred_element_type=f32)
        rank = jnp.sum(hot * (prefix + base), axis=0, keepdims=True).astype(i32)
        base = base + jnp.sum(hot, axis=1, keepdims=True)
        dest = jnp.where(kept, tile * capacity + rank, devices * capacity)
        for h in range(rows // LANES):
            dest_ref[s * (rows // LANES) + h] = dest[:, h * LANES : (h + 1) * LANES]
        offset = off_ref[s : s + 1, :]
        part = rank >> 7
        value = jnp.where(field == part, (offset >> 6) + 1, 0)
        value = jnp.where(field == part + parts, offset & 63, value).astype(f32)
        spread = jnp.concatenate([value] * devices, axis=0)
        stack = jnp.where(tile == owner8, spread, 0.0).astype(bf16)
        spot = (place == (rank & (LANES - 1))).astype(bf16)
        packed = packed + dot_last(stack, spot)
    first = var.astype(bf16).astype(f32)
    second = (var - first).astype(bf16).astype(f32)
    third = var - first - second
    row = iota((devices * META, LANES), 0) & (META - 1)
    packed = jnp.where(row == 4, first, packed)
    packed = jnp.where(row == 5, second, packed)
    packed = jnp.where(row == 6, third, packed)
    meta_ref[...] = packed.astype(bf16)


def own_index():
    return lax.axis_index("expo") * lax.axis_size("fp") + lax.axis_index("fp")


def pack_kernel(raw_ref, above_ref, below_ref, tv_ref, th_ref, dest_ref, meta_ref, all_ref, *rest):
    devices, extended, _ = all_ref.shape
    outs, (edged, vert, conv, spread, stage, sems, *tables) = rest[:devices], rest[devices:]
    me = own_index()
    capacity0 = extended - META
    capacity1 = outs[0].shape[0]
    capacity = capacity0 + capacity1
    rows, cols = raw_ref.shape
    copies = [
        pltpu.make_async_copy(above_ref, edged.at[pl.ds(0, EDGE)], sems.at[0]),
        pltpu.make_async_copy(raw_ref, edged.at[pl.ds(EDGE, rows)], sems.at[1]),
        pltpu.make_async_copy(below_ref, edged.at[pl.ds(EDGE + rows, EDGE)], sems.at[2]),
    ]
    for k, table in enumerate(tables):
        copies.append(pltpu.make_async_copy(dest_ref.at[pl.ds(k, 1)], table, sems.at[3 + k]))
    for copy in copies:
        copy.start()
    vert[:, :LANES] = jnp.zeros((rows, LANES), bf16)
    vert[:, LANES + cols :] = jnp.zeros((rows, LANES), bf16)
    stage[:, capacity0:, :] = meta_ref[...].reshape(devices, META, LANES)
    for copy in copies:
        copy.wait()
    wide = 2 * LANES
    tall = rows + 2 * EDGE
    for c in range(cols // wide):
        part = jnp.dot(tv_ref[:, :tall], edged[:, c * wide : (c + 1) * wide], preferred_element_type=f32)
        vert[:, LANES + c * wide : LANES + (c + 1) * wide] = part.astype(bf16)
    for c in range(cols // wide):
        part = dot_last(vert[:, c * wide : c * wide + 2 * wide], th_ref[...])
        conv[2 * c * rows : (2 * c + 1) * rows, :] = part[:, :LANES]
        conv[(2 * c + 1) * rows : (2 * c + 2) * rows, :] = part[:, LANES:]

    def scatter(r, carry):
        for k, table in enumerate(tables):
            spread[pl.ds(table[0, 0, r], 1), :] = conv[pl.ds(r + k * LANES, 1), :]
        return carry

    lax.fori_loop(0, LANES, scatter, 0, unroll=2)

    def emit(k, carry):
        stage[k, :capacity0, :] = spread[pl.ds(pl.multiple_of(k * capacity, 8), capacity0), :].astype(bf16)
        return carry

    share = devices // 4
    copies = []
    for g in range(4):
        lax.fori_loop(g * share, (g + 1) * share, emit, 0)
        block = pl.ds(g * share, share)
        copies.append(pltpu.make_async_copy(stage.at[block], all_ref.at[block], sems.at[g]))
        copies[-1].start()
    for k, out in enumerate(outs):
        out[...] = spread[pl.ds(pl.multiple_of((me ^ k) * capacity + capacity0, 8), capacity1), :].astype(bf16)
    for copy in copies:
        copy.wait()


def add_rows(tables, scaled, sums, turns, count, first):
    member = iota((GROUP, LANES), 0)
    for p in sorted({p for _, p in tables}):
        low, high = max(first, p * LANES), min(first + count, (p + 1) * LANES)
        for turn in range(turns):

            def rank(r, carry):
                places = [tables[turn * GROUP + k, p][0, 0, r] + (GROUP - k) for k in range(GROUP)]
                start = (r + (turn * count + p * LANES - first)) * GROUP
                fresh = scaled[pl.ds(pl.multiple_of(start, GROUP), GROUP), :]
                held = [acc[pl.ds(place, GROUP), :] for acc, place in zip(sums, places)]
                for k in range(GROUP):
                    sums[k][pl.ds(places[k], GROUP), :] = held[k] + jnp.where(member == k, fresh, 0.0)
                return carry

            lax.fori_loop(low - p * LANES, high - p * LANES, rank, 0, unroll=8)


def first_kernel(slots, parts, values_ref, *refs):
    (spots, factors, weight_out), refs = refs[:3], refs[3:]
    sums, (scaled, sems), refs = refs[:GROUP], refs[GROUP : GROUP + 2], refs[GROUP + 2 :]
    devices, extended, _ = values_ref.shape
    count = extended - META
    used = -(-count // LANES)
    tables = {(n, p): refs[n * used + p] for n in range(devices) for p in range(used)}
    high_id = iota((slots // LANES, LANES), 0)
    low_id = iota((LANES, LANES), 0)
    weight = jnp.zeros((slots // LANES, LANES), f32)
    share = sums[0].shape[0] // devices
    copies = []
    for n in range(devices):
        turn, member = divmod(n, GROUP)
        for acc in sums:
            acc[n * share : (n + 1) * share, :] = jnp.zeros((share, LANES), f32)
        fields = values_ref[n, count:, :].astype(f32)
        factor = fields[4:5, :] + fields[5:6, :] + fields[6:7, :]
        factors[n] = factor
        for p in range(parts):
            high, low = fields[p : p + 1, :], fields[parts + p : parts + p + 1, :]
            slot = jnp.where(high > 0.5, (high - 1.0) * 64.0 + low, float(slots)).astype(i32)
            spots[n * parts + p] = slot
            high = ((slot >> 7) == high_id).astype(bf16)
            low = ((slot & (LANES - 1)) == low_id).astype(bf16)
            weight = weight + factor * dot_last(high, low)
        scaled[pl.ds(turn * count * GROUP + member, count, stride=GROUP), :] = values_ref[n, :count, :].astype(f32) * factor
    for k, ((n, p), table) in enumerate(tables.items()):
        copies.append(pltpu.make_async_copy(spots.at[pl.ds(n * parts + p, 1)], table, sems.at[k]))
        copies[-1].start()
    weight_out[...] = weight
    for copy in copies:
        copy.wait()
    add_rows(tables, scaled, sums, devices // GROUP, count, 0)


def last_kernel(devices, first, parts, *refs):
    values, (spots, factors, weight_in), refs = refs[:devices], refs[devices : devices + 3], refs[devices + 3 + GROUP :]
    (image_ref, weight_ref), sums, refs = refs[:2], refs[2 : 2 + GROUP], refs[2 + GROUP :]
    (scaled, stage, sems), refs = refs[:3], refs[3:]
    count = values[0].shape[0]
    slots = stage.shape[0]
    me = own_index()
    begin = first // LANES
    used = parts - begin
    tables = {(n, begin + p): refs[n * used + p] for n in range(devices) for p in range(used)}
    copies = []
    for k, ((n, p), table) in enumerate(tables.items()):
        copies.append(pltpu.make_async_copy(spots.at[pl.ds((me ^ n) * parts + p, 1)], table, sems.at[k]))
        copies[-1].start()
    copies.append(pltpu.make_async_copy(weight_in, weight_ref, sems.at[len(tables)]))
    copies[-1].start()
    for n in range(devices):
        turn, member = divmod(n, GROUP)
        scaled[pl.ds(turn * count * GROUP + member, count, stride=GROUP), :] = values[n][...].astype(f32) * factors[me ^ n]
    for copy in copies:
        copy.wait()
    add_rows(tables, scaled, sums, devices // GROUP, count, first)
    weight = weight_in[...]

    def mean(h, total):
        scale = jnp.broadcast_to(jnp.maximum(weight[h : h + 1, :], 1.0), (LANES, LANES)).T
        return total / scale

    merge(sums, stage, mean, image_ref, sems)


def merge(sums, stage, finish, out_ref, sems):
    copies = []
    blocks = stage.shape[0] // LANES
    quarter = blocks // 4
    for h in range(blocks):
        total = [acc[GROUP + h * LANES : GROUP + (h + 1) * LANES, :] for acc in sums]
        while len(total) > 1:
            total = [a + b for a, b in zip(total[::2], total[1::2])] + total[len(total) // 2 * 2 :]
        stage[h * LANES : (h + 1) * LANES, :] = finish(h, total[0])
        if h % quarter == quarter - 1:
            ready = pl.ds((h + 1 - quarter) * LANES, quarter * LANES)
            copies.append(pltpu.make_async_copy(stage.at[ready], out_ref.at[ready], sems.at[h // quarter]))
            copies[-1].start()
    for copy in copies:
        copy.wait()


def body(raw_pixels, kernel_bank, kernel_ids, inv_var, gap_start, warp_tile, warp_offset):
    _, rows, cols = raw_pixels.shape
    segs = cols // LANES
    axes = ("expo", "fp")
    devices = lax.axis_size("expo") * lax.axis_size("fp")
    pieces = rows * segs
    capacity = 2 * pieces // devices
    parts = -(-capacity // LANES)
    slots = pieces
    shape = jax.ShapeDtypeStruct

    raw = raw_pixels[0]
    above, below = halo(raw, "fp")
    tiles = jnp.transpose(warp_tile[0], (1, 2, 0))
    offsets = jnp.transpose(warp_offset[0], (1, 0))
    tall = -(-(rows + 2 * EDGE) // LANES) * LANES
    dest, meta, tv, th = pl.pallas_call(
        functools.partial(route_kernel, capacity),
        out_shape=(
            pltpu.VMEM((pieces // LANES, 1, LANES), i32),
            pltpu.VMEM((devices * META, LANES), bf16),
            pltpu.VMEM((rows, tall), bf16),
            pltpu.VMEM((2 * LANES, 4 * LANES), bf16),
        ),
        in_specs=[VMEM] * 6,
        out_specs=(VMEM,) * 4,
        scratch_shapes=[pltpu.VMEM((2, 4 * LANES), f32)],
        cost_estimate=cost(400_000_000, 600_000),
        compiler_params=params(16),
        name="route",
    )(far(tiles), far(offsets), gap_start, inv_var, kernel_ids, far(kernel_bank))

    capacity1 = capacity // 4
    capacity0 = capacity - capacity1
    everything, *sends = pl.pallas_call(
        pack_kernel,
        out_shape=(pltpu.HBM((devices, capacity0 + META, LANES), bf16),)
        + (pltpu.VMEM((capacity1, LANES), bf16),) * devices,
        in_specs=[ANY, ANY, ANY, VMEM, VMEM, VMEM, VMEM],
        out_specs=(ANY,) + (VMEM,) * devices,
        scratch_shapes=[
            pltpu.VMEM((rows + 2 * EDGE, cols), bf16),
            pltpu.VMEM((rows, cols + 2 * LANES), bf16),
            pltpu.VMEM((pieces, LANES), f32),
            pltpu.VMEM((devices * capacity + 8, LANES), f32),
            pltpu.VMEM((devices, capacity0 + META, LANES), bf16),
            pltpu.SemaphoreType.DMA((3 + pieces // LANES,)),
        ]
        + [pltpu.SMEM((1, 1, LANES), i32)] * (pieces // LANES),
        cost_estimate=cost(10_000_000_000, 4_000_000),
        compiler_params=params(20),
        name="pack",
    )(far(raw), near(above), near(below), near(tv), near(th), near(dest), near(meta))

    most = 8 * devices
    total = pltpu.VMEM((-(-(slots + 3 * GROUP) // most) * most, LANES), f32)
    with jax.named_scope("every"):
        got = lax.all_to_all(everything, axes, split_axis=0, concat_axis=0, tiled=True)
    rest = [sends[0]]
    with jax.named_scope("rest"):
        for k in range(1, devices):
            rest.append(lax.ppermute(sends[k], axes, [(i, i ^ k) for i in range(devices)]))

    used = -(-capacity0 // LANES)
    spots, factors, weight, *sums = pl.pallas_call(
        functools.partial(first_kernel, slots, parts),
        out_shape=(
            pltpu.VMEM((devices * parts, 1, LANES), i32),
            pltpu.VMEM((devices, 1, LANES), f32),
            pltpu.VMEM((slots // LANES, LANES), f32),
        )
        + (total,) * GROUP,
        in_specs=[VMEM],
        out_specs=(VMEM,) * (3 + GROUP),
        scratch_shapes=[pltpu.VMEM((devices * capacity0, LANES), f32), pltpu.SemaphoreType.DMA((devices * used,))]
        + [pltpu.SMEM((1, 1, LANES), i32)] * (devices * used),
        cost_estimate=cost(4_000_000_000, 8_000_000),
        compiler_params=params(8),
        name="sum_first",
    )(near(got))
    used = parts - capacity0 // LANES
    image, weight, *_ = pl.pallas_call(
        functools.partial(last_kernel, devices, capacity0, parts),
        out_shape=(pltpu.HBM((slots, LANES), f32), pltpu.HBM((slots // LANES, LANES), f32)) + (total,) * GROUP,
        in_specs=[VMEM] * (devices + 3 + GROUP),
        out_specs=(ANY, ANY) + (VMEM,) * GROUP,
        scratch_shapes=[
            pltpu.VMEM((devices * capacity1, LANES), f32),
            pltpu.VMEM((slots, LANES), f32),
            pltpu.SemaphoreType.DMA((devices * used + 1,)),
        ]
        + [pltpu.SMEM((1, 1, LANES), i32)] * (devices * used),
        input_output_aliases={devices + 3 + k: 2 + k for k in range(GROUP)},
        cost_estimate=cost(4_000_000_000, 8_000_000),
        compiler_params=params(8),
        name="sum_last",
    )(*[near(x) for x in rest], near(spots), near(factors), near(weight), *[near(x) for x in sums])
    return image[None], weight.reshape(1, slots)


def solution(mesh):
    in_specs = (
        P("expo", "fp", None),
        P(),
        P("expo", "fp"),
        P("expo", "fp"),
        P("expo", "fp"),
        P("expo", "fp", None, None),
        P("expo", "fp", None),
    )
    out_specs = (P(("expo", "fp"), None, None), P(("expo", "fp"), None))
    return jax.shard_map(body, mesh=mesh, in_specs=in_specs, out_specs=out_specs, check_vma=False)
```

```python
import functools

import jax
import jax.numpy as jnp
from jax import lax
from jax.experimental import pallas as pl
from jax.experimental.pallas import tpu as pltpu
from jax.sharding import PartitionSpec as P

GAP = 32
EDGE = 32
LANES = 128
META = 8
GROUP = 8


VMEM = pl.BlockSpec(memory_space=pltpu.VMEM)
ANY = pl.BlockSpec(memory_space=pl.ANY)
f32, bf16, i32 = jnp.float32, jnp.bfloat16, jnp.int32


def iota(shape, dim):
    return lax.broadcasted_iota(i32, shape, dim)


def dot_last(a, b):
    return lax.dot_general(a, b, (((1,), (1,)), ((), ())), preferred_element_type=f32)


def near(x):
    return pltpu.with_memory_space_constraint(x, pltpu.VMEM)


def far(x):
    return pltpu.with_memory_space_constraint(x, pltpu.HBM)


def params(mib):
    return pltpu.CompilerParams(vmem_limit_bytes=mib << 20)


def cost(flops, moved):
    return pl.CostEstimate(flops=flops, bytes_accessed=moved, transcendentals=0)


def halo(shard, axis):
    size = lax.axis_size(axis)
    up = [(i, i + 1) for i in range(size - 1)]
    down = [(i + 1, i) for i in range(size - 1)]
    above = lax.ppermute(shard[-EDGE:], axis, up)
    below = lax.ppermute(shard[:EDGE], axis, down)
    return above, below


def route_kernel(capacity, tile_ref, off_ref, gap_ref, var_ref, id_ref, bank_ref, dest_ref, meta_ref, tv_ref, th_ref, line_ref):
    segs, rows = off_ref.shape
    devices = meta_ref.shape[0] // META
    parts = -(-capacity // LANES)
    gap, var, which_bank = gap_ref[...], var_ref[...], id_ref[...]
    bank = bank_ref[...].astype(f32)
    chosen = jnp.where(which_bank == 0, bank[0], 0.0)
    for k in range(1, bank.shape[0]):
        chosen = jnp.where(which_bank == k, bank[k], chosen)
    taps = bank.shape[2]
    half = taps // 2
    lead = -half % 8
    line_ref[...] = jnp.zeros(line_ref.shape, f32)
    line_ref[:, lead : lead + taps] = chosen
    for ref, which, shift in ((tv_ref, 0, EDGE - half), (th_ref, 1, LANES - half)):
        height, width = ref.shape
        wide = jnp.broadcast_to(line_ref[which : which + 1, :width], (height, width))
        ref[...] = pltpu.roll(wide, shift - lead, 1, stride=1, stride_axis=0).astype(bf16)
    line = iota((1, rows), 1)
    kept = jnp.logical_or(line < gap, line >= gap + GAP)
    before = (iota((rows, rows), 0) < iota((rows, rows), 1)).astype(bf16)
    owner = iota((devices, rows), 0)
    owner8 = iota((devices * META, rows), 0) >> 3
    field = iota((META, rows), 0)
    place = iota((LANES, rows), 0)
    base = jnp.zeros((devices, 1), f32)
    packed = jnp.zeros((devices * META, LANES), f32)
    for s in range(segs):
        tile = jnp.where(kept, tile_ref[s], -1)
        hot = (tile == owner).astype(f32)
        prefix = jnp.dot(hot.astype(bf16), before, preferred_element_type=f32)
        rank = jnp.sum(hot * (prefix + base), axis=0, keepdims=True).astype(i32)
        base = base + jnp.sum(hot, axis=1, keepdims=True)
        dest = jnp.where(kept, tile * capacity + rank, devices * capacity)
        for h in range(rows // LANES):
            dest_ref[s * (rows // LANES) + h] = dest[:, h * LANES : (h + 1) * LANES]
        offset = off_ref[s : s + 1, :]
        part = rank >> 7
        value = jnp.where(field == part, (offset >> 6) + 1, 0)
        value = jnp.where(field == part + parts, offset & 63, value).astype(f32)
        spread = jnp.concatenate([value] * devices, axis=0)
        stack = jnp.where(tile == owner8, spread, 0.0).astype(bf16)
        spot = (place == (rank & (LANES - 1))).astype(bf16)
        packed = packed + dot_last(stack, spot)
    first = var.astype(bf16).astype(f32)
    second = (var - first).astype(bf16).astype(f32)
    third = var - first - second
    row = iota((devices * META, LANES), 0) & (META - 1)
    packed = jnp.where(row == 4, first, packed)
    packed = jnp.where(row == 5, second, packed)
    packed = jnp.where(row == 6, third, packed)
    meta_ref[...] = packed.astype(bf16)


def own_index():
    return lax.axis_index("expo") * lax.axis_size("fp") + lax.axis_index("fp")


def pack_kernel(raw_ref, above_ref, below_ref, tv_ref, th_ref, dest_ref, meta_ref, all_ref, keep_ref, give_ref, edged, vert, conv, spread, stage, sems, *tables):
    devices, extended, _ = all_ref.shape
    me = own_index()
    capacity0 = extended - META
    chips, capacity1, _ = keep_ref.shape
    capacity = capacity0 + capacity1
    rows, cols = raw_ref.shape
    copies = [
        pltpu.make_async_copy(above_ref, edged.at[pl.ds(0, EDGE)], sems.at[0]),
        pltpu.make_async_copy(raw_ref, edged.at[pl.ds(EDGE, rows)], sems.at[1]),
        pltpu.make_async_copy(below_ref, edged.at[pl.ds(EDGE + rows, EDGE)], sems.at[2]),
    ]
    for k, table in enumerate(tables):
        copies.append(pltpu.make_async_copy(dest_ref.at[pl.ds(k, 1)], table, sems.at[3 + k]))
    for copy in copies:
        copy.start()
    vert[:, :LANES] = jnp.zeros((rows, LANES), bf16)
    vert[:, LANES + cols :] = jnp.zeros((rows, LANES), bf16)
    stage[:, capacity0:, :] = meta_ref[...].reshape(devices, META, LANES)
    for copy in copies:
        copy.wait()
    wide = 2 * LANES
    tall = rows + 2 * EDGE
    for c in range(cols // wide):
        part = jnp.dot(tv_ref[:, :tall], edged[:, c * wide : (c + 1) * wide], preferred_element_type=f32)
        vert[:, LANES + c * wide : LANES + (c + 1) * wide] = part.astype(bf16)
    for c in range(cols // wide):
        part = dot_last(vert[:, c * wide : c * wide + 2 * wide], th_ref[...])
        conv[2 * c * rows : (2 * c + 1) * rows, :] = part[:, :LANES]
        conv[(2 * c + 1) * rows : (2 * c + 2) * rows, :] = part[:, LANES:]

    def scatter(r, carry):
        for k, table in enumerate(tables):
            spread[pl.ds(table[0, 0, r], 1), :] = conv[pl.ds(r + k * LANES, 1), :]
        return carry

    lax.fori_loop(0, LANES, scatter, 0, unroll=2)

    def emit(k, carry):
        stage[k, :capacity0, :] = spread[pl.ds(pl.multiple_of(k * capacity, 8), capacity0), :].astype(bf16)
        return carry

    share = devices // 4
    copies = []
    for g in range(4):
        lax.fori_loop(g * share, (g + 1) * share, emit, 0)
        block = pl.ds(g * share, share)
        copies.append(pltpu.make_async_copy(stage.at[block], all_ref.at[block], sems.at[g]))
        copies[-1].start()
    for j in range(chips):
        for out, k in ((keep_ref, 2 * j), (give_ref, 2 * j + 1)):
            out[j] = spread[pl.ds(pl.multiple_of((me ^ k) * capacity + capacity0, 8), capacity1), :].astype(bf16)
    for copy in copies:
        copy.wait()


def join_kernel(keep_ref, take_ref, *outs):
    count = keep_ref.shape[1]
    for j, out in enumerate(outs):
        out[:count, :] = keep_ref[j]
        out[count:, :] = take_ref[j]


def add_rows(tables, scaled, sums, turns, count, first):
    member = iota((GROUP, LANES), 0)
    for p in sorted({p for _, p in tables}):
        low, high = max(first, p * LANES), min(first + count, (p + 1) * LANES)
        for turn in range(turns):

            def rank(r, carry):
                places = [tables[turn * GROUP + k, p][0, 0, r] + (GROUP - k) for k in range(GROUP)]
                start = (r + (turn * count + p * LANES - first)) * GROUP
                fresh = scaled[pl.ds(pl.multiple_of(start, GROUP), GROUP), :]
                held = [acc[pl.ds(place, GROUP), :] for acc, place in zip(sums, places)]
                for k in range(GROUP):
                    sums[k][pl.ds(places[k], GROUP), :] = held[k] + jnp.where(member == k, fresh, 0.0)
                return carry

            lax.fori_loop(low - p * LANES, high - p * LANES, rank, 0, unroll=8)


def first_kernel(slots, parts, values_ref, *refs):
    (spots, factors, weight_out), refs = refs[:3], refs[3:]
    sums, (scaled, sems), refs = refs[:GROUP], refs[GROUP : GROUP + 2], refs[GROUP + 2 :]
    devices, extended, _ = values_ref.shape
    count = extended - META
    used = -(-count // LANES)
    tables = {(n, p): refs[n * used + p] for n in range(devices) for p in range(used)}
    high_id = iota((slots // LANES, LANES), 0)
    low_id = iota((LANES, LANES), 0)
    weight = jnp.zeros((slots // LANES, LANES), f32)
    share = sums[0].shape[0] // devices
    copies = []
    for n in range(devices):
        turn, member = divmod(n, GROUP)
        for acc in sums:
            acc[n * share : (n + 1) * share, :] = jnp.zeros((share, LANES), f32)
        fields = values_ref[n, count:, :].astype(f32)
        factor = fields[4:5, :] + fields[5:6, :] + fields[6:7, :]
        factors[n] = factor
        for p in range(parts):
            high, low = fields[p : p + 1, :], fields[parts + p : parts + p + 1, :]
            slot = jnp.where(high > 0.5, (high - 1.0) * 64.0 + low, float(slots)).astype(i32)
            spots[n * parts + p] = slot
            high = ((slot >> 7) == high_id).astype(bf16)
            low = ((slot & (LANES - 1)) == low_id).astype(bf16)
            weight = weight + factor * dot_last(high, low)
        scaled[pl.ds(turn * count * GROUP + member, count, stride=GROUP), :] = values_ref[n, :count, :].astype(f32) * factor
    for k, ((n, p), table) in enumerate(tables.items()):
        copies.append(pltpu.make_async_copy(spots.at[pl.ds(n * parts + p, 1)], table, sems.at[k]))
        copies[-1].start()
    weight_out[...] = weight
    for copy in copies:
        copy.wait()
    add_rows(tables, scaled, sums, devices // GROUP, count, 0)


def last_kernel(devices, first, parts, *refs):
    chips = devices // 2
    pairs, (spots, factors, weight_in), refs = refs[:chips], refs[chips : chips + 3], refs[chips + 3 + GROUP :]
    (image_ref, weight_ref), sums, refs = refs[:2], refs[2 : 2 + GROUP], refs[2 + GROUP :]
    (scaled, stage, sems), refs = refs[:3], refs[3:]
    count = pairs[0].shape[0] // 2
    slots = stage.shape[0]
    me = own_index()
    begin = first // LANES
    used = parts - begin
    tables = {(n, begin + p): refs[n * used + p] for n in range(devices) for p in range(used)}
    copies = []
    for k, ((n, p), table) in enumerate(tables.items()):
        copies.append(pltpu.make_async_copy(spots.at[pl.ds((me ^ n) * parts + p, 1)], table, sems.at[k]))
        copies[-1].start()
    copies.append(pltpu.make_async_copy(weight_in, weight_ref, sems.at[len(tables)]))
    copies[-1].start()
    for n in range(devices):
        turn, member = divmod(n, GROUP)
        scaled[pl.ds(turn * count * GROUP + member, count, stride=GROUP), :] = pairs[n // 2][n % 2 * count : (n % 2 + 1) * count, :].astype(f32) * factors[me ^ n]
    for copy in copies:
        copy.wait()
    add_rows(tables, scaled, sums, devices // GROUP, count, first)
    weight = weight_in[...]

    def mean(h, total):
        scale = jnp.broadcast_to(jnp.maximum(weight[h : h + 1, :], 1.0), (LANES, LANES)).T
        return total / scale

    merge(sums, stage, mean, image_ref, sems)


def merge(sums, stage, finish, out_ref, sems):
    copies = []
    blocks = stage.shape[0] // LANES
    quarter = blocks // 4
    for h in range(blocks):
        total = [acc[GROUP + h * LANES : GROUP + (h + 1) * LANES, :] for acc in sums]
        while len(total) > 1:
            total = [a + b for a, b in zip(total[::2], total[1::2])] + total[len(total) // 2 * 2 :]
        stage[h * LANES : (h + 1) * LANES, :] = finish(h, total[0])
        if h % quarter == quarter - 1:
            ready = pl.ds((h + 1 - quarter) * LANES, quarter * LANES)
            copies.append(pltpu.make_async_copy(stage.at[ready], out_ref.at[ready], sems.at[h // quarter]))
            copies[-1].start()
    for copy in copies:
        copy.wait()


def body(raw_pixels, kernel_bank, kernel_ids, inv_var, gap_start, warp_tile, warp_offset):
    _, rows, cols = raw_pixels.shape
    segs = cols // LANES
    axes = ("expo", "fp")
    devices = lax.axis_size("expo") * lax.axis_size("fp")
    pieces = rows * segs
    capacity = 2 * pieces // devices
    parts = -(-capacity // LANES)
    slots = pieces
    shape = jax.ShapeDtypeStruct

    raw = raw_pixels[0]
    above, below = halo(raw, "fp")
    tiles = jnp.transpose(warp_tile[0], (1, 2, 0))
    offsets = jnp.transpose(warp_offset[0], (1, 0))
    tall = -(-(rows + 2 * EDGE) // LANES) * LANES
    dest, meta, tv, th = pl.pallas_call(
        functools.partial(route_kernel, capacity),
        out_shape=(
            pltpu.VMEM((pieces // LANES, 1, LANES), i32),
            pltpu.VMEM((devices * META, LANES), bf16),
            pltpu.VMEM((rows, tall), bf16),
            pltpu.VMEM((2 * LANES, 4 * LANES), bf16),
        ),
        in_specs=[VMEM] * 6,
        out_specs=(VMEM,) * 4,
        scratch_shapes=[pltpu.VMEM((2, 4 * LANES), f32)],
        cost_estimate=cost(400_000_000, 600_000),
        compiler_params=params(16),
        name="route",
    )(far(tiles), far(offsets), gap_start, inv_var, kernel_ids, far(kernel_bank))

    capacity1 = capacity // 4
    capacity0 = capacity - capacity1
    chips = devices // 2
    everything, keep, give = pl.pallas_call(
        pack_kernel,
        out_shape=(pltpu.HBM((devices, capacity0 + META, LANES), bf16),)
        + (pltpu.VMEM((chips, capacity1, LANES), bf16),) * 2,
        in_specs=[ANY, ANY, ANY, VMEM, VMEM, VMEM, VMEM],
        out_specs=(ANY, VMEM, VMEM),
        scratch_shapes=[
            pltpu.VMEM((rows + 2 * EDGE, cols), bf16),
            pltpu.VMEM((rows, cols + 2 * LANES), bf16),
            pltpu.VMEM((pieces, LANES), f32),
            pltpu.VMEM((devices * capacity + 8, LANES), f32),
            pltpu.VMEM((devices, capacity0 + META, LANES), bf16),
            pltpu.SemaphoreType.DMA((3 + pieces // LANES,)),
        ]
        + [pltpu.SMEM((1, 1, LANES), i32)] * (pieces // LANES),
        cost_estimate=cost(10_000_000_000, 4_000_000),
        compiler_params=params(20),
        name="pack",
    )(far(raw), near(above), near(below), near(tv), near(th), near(dest), near(meta))

    most = 8 * devices
    total = pltpu.VMEM((-(-(slots + 3 * GROUP) // most) * most, LANES), f32)
    with jax.named_scope("every"):
        got = lax.all_to_all(everything, axes, split_axis=0, concat_axis=0, tiled=True)
    with jax.named_scope("swap"):
        take = lax.ppermute(give, axes, [(i, i ^ 1) for i in range(devices)])
    joined = pl.pallas_call(
        join_kernel,
        out_shape=(pltpu.VMEM((2 * capacity1, LANES), bf16),) * chips,
        in_specs=[VMEM, VMEM],
        out_specs=(VMEM,) * chips,
        cost_estimate=cost(1_000_000, 1_000_000),
        compiler_params=params(2),
        name="join",
    )(near(keep), near(take))
    rest = [joined[0]]
    with jax.named_scope("rest"):
        for j in range(1, chips):
            rest.append(lax.ppermute(joined[j], axes, [(i, i ^ (2 * j)) for i in range(devices)]))

    used = -(-capacity0 // LANES)
    spots, factors, weight, *sums = pl.pallas_call(
        functools.partial(first_kernel, slots, parts),
        out_shape=(
            pltpu.VMEM((devices * parts, 1, LANES), i32),
            pltpu.VMEM((devices, 1, LANES), f32),
            pltpu.VMEM((slots // LANES, LANES), f32),
        )
        + (total,) * GROUP,
        in_specs=[VMEM],
        out_specs=(VMEM,) * (3 + GROUP),
        scratch_shapes=[pltpu.VMEM((devices * capacity0, LANES), f32), pltpu.SemaphoreType.DMA((devices * used,))]
        + [pltpu.SMEM((1, 1, LANES), i32)] * (devices * used),
        cost_estimate=cost(4_000_000_000, 8_000_000),
        compiler_params=params(8),
        name="sum_first",
    )(near(got))
    used = parts - capacity0 // LANES
    image, weight, *_ = pl.pallas_call(
        functools.partial(last_kernel, devices, capacity0, parts),
        out_shape=(pltpu.HBM((slots, LANES), f32), pltpu.HBM((slots // LANES, LANES), f32)) + (total,) * GROUP,
        in_specs=[VMEM] * (chips + 3 + GROUP),
        out_specs=(ANY, ANY) + (VMEM,) * GROUP,
        scratch_shapes=[
            pltpu.VMEM((devices * capacity1, LANES), f32),
            pltpu.VMEM((slots, LANES), f32),
            pltpu.SemaphoreType.DMA((devices * used + 1,)),
        ]
        + [pltpu.SMEM((1, 1, LANES), i32)] * (devices * used),
        input_output_aliases={chips + 3 + k: 2 + k for k in range(GROUP)},
        cost_estimate=cost(4_000_000_000, 8_000_000),
        compiler_params=params(8),
        name="sum_last",
    )(*[near(x) for x in rest], near(spots), near(factors), near(weight), *[near(x) for x in sums])
    return image[None], weight.reshape(1, slots)


def solution(mesh):
    in_specs = (
        P("expo", "fp", None),
        P(),
        P("expo", "fp"),
        P("expo", "fp"),
        P("expo", "fp"),
        P("expo", "fp", None, None),
        P("expo", "fp", None),
    )
    out_specs = (P(("expo", "fp"), None, None), P(("expo", "fp"), None))
    return jax.shard_map(body, mesh=mesh, in_specs=in_specs, out_specs=out_specs, check_vma=False)
```

```python
import functools

import jax
import jax.numpy as jnp
from jax import lax
from jax.experimental import pallas as pl
from jax.experimental.pallas import tpu as pltpu
from jax.sharding import PartitionSpec as P

GAP = 32
EDGE = 32
LANES = 128
META = 8
GROUP = 8


VMEM = pl.BlockSpec(memory_space=pltpu.VMEM)
ANY = pl.BlockSpec(memory_space=pl.ANY)
f32, bf16, i32 = jnp.float32, jnp.bfloat16, jnp.int32


def iota(shape, dim):
    return lax.broadcasted_iota(i32, shape, dim)


def dot_last(a, b):
    return lax.dot_general(a, b, (((1,), (1,)), ((), ())), preferred_element_type=f32)


def near(x):
    return pltpu.with_memory_space_constraint(x, pltpu.VMEM)


def far(x):
    return pltpu.with_memory_space_constraint(x, pltpu.HBM)


def params(mib):
    return pltpu.CompilerParams(vmem_limit_bytes=mib << 20)


def cost(flops, moved):
    return pl.CostEstimate(flops=flops, bytes_accessed=moved, transcendentals=0)


def halo(shard, axis):
    size = lax.axis_size(axis)
    up = [(i, i + 1) for i in range(size - 1)]
    down = [(i + 1, i) for i in range(size - 1)]
    above = lax.ppermute(shard[-EDGE:], axis, up)
    below = lax.ppermute(shard[:EDGE], axis, down)
    return above, below


def route_kernel(capacity, tile_ref, off_ref, gap_ref, var_ref, id_ref, bank_ref, dest_ref, meta_ref, tv_ref, th_ref, line_ref):
    segs, rows = off_ref.shape
    devices = meta_ref.shape[0] // META
    parts = -(-capacity // LANES)
    gap, var, which_bank = gap_ref[...], var_ref[...], id_ref[...]
    bank = bank_ref[...].astype(f32)
    chosen = jnp.where(which_bank == 0, bank[0], 0.0)
    for k in range(1, bank.shape[0]):
        chosen = jnp.where(which_bank == k, bank[k], chosen)
    taps = bank.shape[2]
    half = taps // 2
    lead = -half % 8
    line_ref[...] = jnp.zeros(line_ref.shape, f32)
    line_ref[:, lead : lead + taps] = chosen
    for ref, which, shift in ((tv_ref, 0, EDGE - half), (th_ref, 1, LANES - half)):
        height, width = ref.shape
        wide = jnp.broadcast_to(line_ref[which : which + 1, :width], (height, width))
        ref[...] = pltpu.roll(wide, shift - lead, 1, stride=1, stride_axis=0).astype(bf16)
    line = iota((1, rows), 1)
    kept = jnp.logical_or(line < gap, line >= gap + GAP)
    before = (iota((rows, rows), 0) < iota((rows, rows), 1)).astype(bf16)
    owner = iota((devices, rows), 0)
    owner8 = iota((devices * META, rows), 0) >> 3
    field = iota((META, rows), 0)
    place = iota((LANES, rows), 0)
    base = jnp.zeros((devices, 1), f32)
    packed = jnp.zeros((devices * META, LANES), f32)
    for s in range(segs):
        tile = jnp.where(kept, tile_ref[s], -1)
        hot = (tile == owner).astype(f32)
        prefix = jnp.dot(hot.astype(bf16), before, preferred_element_type=f32)
        rank = jnp.sum(hot * (prefix + base), axis=0, keepdims=True).astype(i32)
        base = base + jnp.sum(hot, axis=1, keepdims=True)
        dest = jnp.where(kept, tile * capacity + rank, devices * capacity)
        for h in range(rows // LANES):
            dest_ref[s * (rows // LANES) + h] = dest[:, h * LANES : (h + 1) * LANES]
        offset = off_ref[s : s + 1, :]
        part = rank >> 7
        value = jnp.where(field == part, (offset >> 6) + 1, 0)
        value = jnp.where(field == part + parts, offset & 63, value).astype(f32)
        spread = jnp.concatenate([value] * devices, axis=0)
        stack = jnp.where(tile == owner8, spread, 0.0).astype(bf16)
        spot = (place == (rank & (LANES - 1))).astype(bf16)
        packed = packed + dot_last(stack, spot)
    first = var.astype(bf16).astype(f32)
    second = (var - first).astype(bf16).astype(f32)
    third = var - first - second
    row = iota((devices * META, LANES), 0) & (META - 1)
    packed = jnp.where(row == 4, first, packed)
    packed = jnp.where(row == 5, second, packed)
    packed = jnp.where(row == 6, third, packed)
    meta_ref[...] = packed.astype(bf16)


def own_index():
    return lax.axis_index("expo") * lax.axis_size("fp") + lax.axis_index("fp")


def pack_kernel(raw_ref, above_ref, below_ref, tv_ref, th_ref, dest_ref, meta_ref, all_ref, keep_ref, give_ref, edged, vert, conv, spread, stage, sems, *tables):
    devices, extended, _ = all_ref.shape
    me = own_index()
    capacity0 = extended - META
    chips, capacity1, _ = keep_ref.shape
    capacity = capacity0 + capacity1
    rows, cols = raw_ref.shape
    copies = [
        pltpu.make_async_copy(above_ref, edged.at[pl.ds(0, EDGE)], sems.at[0]),
        pltpu.make_async_copy(raw_ref, edged.at[pl.ds(EDGE, rows)], sems.at[1]),
        pltpu.make_async_copy(below_ref, edged.at[pl.ds(EDGE + rows, EDGE)], sems.at[2]),
    ]
    for k, table in enumerate(tables):
        copies.append(pltpu.make_async_copy(dest_ref.at[pl.ds(k, 1)], table, sems.at[3 + k]))
    for copy in copies:
        copy.start()
    vert[:, :LANES] = jnp.zeros((rows, LANES), bf16)
    vert[:, LANES + cols :] = jnp.zeros((rows, LANES), bf16)
    stage[:, capacity0:, :] = meta_ref[...].reshape(devices, META, LANES)
    for copy in copies:
        copy.wait()
    wide = 2 * LANES
    tall = rows + 2 * EDGE
    for c in range(cols // wide):
        part = jnp.dot(tv_ref[:, :tall], edged[:, c * wide : (c + 1) * wide], preferred_element_type=f32)
        vert[:, LANES + c * wide : LANES + (c + 1) * wide] = part.astype(bf16)
    for c in range(cols // wide):
        part = dot_last(vert[:, c * wide : c * wide + 2 * wide], th_ref[...])
        conv[2 * c * rows : (2 * c + 1) * rows, :] = part[:, :LANES]
        conv[(2 * c + 1) * rows : (2 * c + 2) * rows, :] = part[:, LANES:]

    def scatter(r, carry):
        for k, table in enumerate(tables):
            spread[pl.ds(table[0, 0, r], 1), :] = conv[pl.ds(r + k * LANES, 1), :]
        return carry

    lax.fori_loop(0, LANES, scatter, 0, unroll=2)

    def emit(k, carry):
        stage[k, :capacity0, :] = spread[pl.ds(pl.multiple_of(k * capacity, 8), capacity0), :].astype(bf16)
        return carry

    share = devices // 4
    copies = []
    for g in range(4):
        lax.fori_loop(g * share, (g + 1) * share, emit, 0)
        block = pl.ds(g * share, share)
        copies.append(pltpu.make_async_copy(stage.at[block], all_ref.at[block], sems.at[g]))
        copies[-1].start()
    for j in range(chips):
        for out, k in ((keep_ref, 2 * j), (give_ref, 2 * j + 1)):
            out[j] = spread[pl.ds(pl.multiple_of((me ^ k) * capacity + capacity0, 8), capacity1), :].astype(bf16)
    for copy in copies:
        copy.wait()


def join_kernel(keep_ref, take_ref, *outs):
    count = keep_ref.shape[1]
    for j, out in enumerate(outs):
        out[:count, :] = keep_ref[j]
        out[count:, :] = take_ref[j]


def add_rows(tables, scaled, sums, turns, count, first):
    member = iota((GROUP, LANES), 0)
    for p in sorted({p for _, p in tables}):
        low, high = max(first, p * LANES), min(first + count, (p + 1) * LANES)
        for turn in range(turns):

            def rank(r, carry):
                places = [tables[turn * GROUP + k, p][0, 0, r] for k in range(GROUP)]
                start = (r + (turn * count + p * LANES - first)) * GROUP
                fresh = scaled[pl.ds(pl.multiple_of(start, GROUP), GROUP), :]
                held = [acc[pl.ds(place, GROUP), :] for acc, place in zip(sums, places)]
                for k in range(GROUP):
                    sums[k][pl.ds(places[k], GROUP), :] = held[k] + jnp.where(member == k, fresh, 0.0)
                return carry

            lax.fori_loop(low - p * LANES, high - p * LANES, rank, 0, unroll=8)


def first_kernel(slots, parts, values_ref, *refs):
    (spots, factors, weight_out), refs = refs[:3], refs[3:]
    sums, (scaled, shifted, sems), refs = refs[:GROUP], refs[GROUP : GROUP + 3], refs[GROUP + 3 :]
    devices, extended, _ = values_ref.shape
    count = extended - META
    used = -(-count // LANES)
    tables = {(n, p): refs[n * used + p] for n in range(devices) for p in range(used)}
    high_id = iota((slots // LANES, LANES), 0)
    low_id = iota((LANES, LANES), 0)
    weight = jnp.zeros((slots // LANES, LANES), f32)
    share = sums[0].shape[0] // devices
    copies = []
    for n in range(devices):
        turn, member = divmod(n, GROUP)
        for acc in sums:
            acc[n * share : (n + 1) * share, :] = jnp.zeros((share, LANES), f32)
        fields = values_ref[n, count:, :].astype(f32)
        factor = fields[4:5, :] + fields[5:6, :] + fields[6:7, :]
        factors[n] = factor
        for p in range(parts):
            high, low = fields[p : p + 1, :], fields[parts + p : parts + p + 1, :]
            slot = jnp.where(high > 0.5, (high - 1.0) * 64.0 + low, float(slots)).astype(i32)
            spots[n * parts + p] = slot
            if p < used:
                shifted[n * used + p] = slot + (GROUP - member)
            high = ((slot >> 7) == high_id).astype(bf16)
            low = ((slot & (LANES - 1)) == low_id).astype(bf16)
            weight = weight + factor * dot_last(high, low)
        scaled[pl.ds(turn * count * GROUP + member, count, stride=GROUP), :] = values_ref[n, :count, :].astype(f32) * factor
    for k, table in enumerate(tables.values()):
        copies.append(pltpu.make_async_copy(shifted.at[pl.ds(k, 1)], table, sems.at[k]))
        copies[-1].start()
    weight_out[...] = weight
    for copy in copies:
        copy.wait()
    add_rows(tables, scaled, sums, devices // GROUP, count, 0)


def last_kernel(devices, first, parts, *refs):
    chips = devices // 2
    pairs, (spots, factors, weight_in), refs = refs[:chips], refs[chips : chips + 3], refs[chips + 3 + GROUP :]
    (image_ref, weight_ref), sums, refs = refs[:2], refs[2 : 2 + GROUP], refs[2 + GROUP :]
    (scaled, shifted, stage, sems), refs = refs[:4], refs[4:]
    count = pairs[0].shape[0] // 2
    slots = stage.shape[0]
    me = own_index()
    begin = first // LANES
    used = parts - begin
    tables = {(n, begin + p): refs[n * used + p] for n in range(devices) for p in range(used)}
    copies = []
    for k, (n, p) in enumerate(tables):
        shifted[k] = spots[(me ^ n) * parts + p] + (GROUP - n % GROUP)
    for k, table in enumerate(tables.values()):
        copies.append(pltpu.make_async_copy(shifted.at[pl.ds(k, 1)], table, sems.at[k]))
        copies[-1].start()
    copies.append(pltpu.make_async_copy(weight_in, weight_ref, sems.at[len(tables)]))
    copies[-1].start()
    for n in range(devices):
        turn, member = divmod(n, GROUP)
        scaled[pl.ds(turn * count * GROUP + member, count, stride=GROUP), :] = pairs[n // 2][n % 2 * count : (n % 2 + 1) * count, :].astype(f32) * factors[me ^ n]
    for copy in copies:
        copy.wait()
    add_rows(tables, scaled, sums, devices // GROUP, count, first)
    weight = weight_in[...]

    def mean(h, total):
        scale = jnp.broadcast_to(jnp.maximum(weight[h : h + 1, :], 1.0), (LANES, LANES)).T
        return total / scale

    merge(sums, stage, mean, image_ref, sems)


def merge(sums, stage, finish, out_ref, sems):
    copies = []
    blocks = stage.shape[0] // LANES
    quarter = blocks // 4
    for h in range(blocks):
        total = [acc[GROUP + h * LANES : GROUP + (h + 1) * LANES, :] for acc in sums]
        while len(total) > 1:
            total = [a + b for a, b in zip(total[::2], total[1::2])] + total[len(total) // 2 * 2 :]
        stage[h * LANES : (h + 1) * LANES, :] = finish(h, total[0])
        if h % quarter == quarter - 1:
            ready = pl.ds((h + 1 - quarter) * LANES, quarter * LANES)
            copies.append(pltpu.make_async_copy(stage.at[ready], out_ref.at[ready], sems.at[h // quarter]))
            copies[-1].start()
    for copy in copies:
        copy.wait()


def body(raw_pixels, kernel_bank, kernel_ids, inv_var, gap_start, warp_tile, warp_offset):
    _, rows, cols = raw_pixels.shape
    segs = cols // LANES
    axes = ("expo", "fp")
    devices = lax.axis_size("expo") * lax.axis_size("fp")
    pieces = rows * segs
    capacity = 2 * pieces // devices
    parts = -(-capacity // LANES)
    slots = pieces
    shape = jax.ShapeDtypeStruct

    raw = raw_pixels[0]
    above, below = halo(raw, "fp")
    tiles = jnp.transpose(warp_tile[0], (1, 2, 0))
    offsets = jnp.transpose(warp_offset[0], (1, 0))
    tall = -(-(rows + 2 * EDGE) // LANES) * LANES
    dest, meta, tv, th = pl.pallas_call(
        functools.partial(route_kernel, capacity),
        out_shape=(
            pltpu.VMEM((pieces // LANES, 1, LANES), i32),
            pltpu.VMEM((devices * META, LANES), bf16),
            pltpu.VMEM((rows, tall), bf16),
            pltpu.VMEM((2 * LANES, 4 * LANES), bf16),
        ),
        in_specs=[VMEM] * 6,
        out_specs=(VMEM,) * 4,
        scratch_shapes=[pltpu.VMEM((2, 4 * LANES), f32)],
        cost_estimate=cost(400_000_000, 600_000),
        compiler_params=params(16),
        name="route",
    )(far(tiles), far(offsets), gap_start, inv_var, kernel_ids, far(kernel_bank))

    capacity1 = capacity * 3 // 8
    capacity0 = capacity - capacity1
    chips = devices // 2
    everything, keep, give = pl.pallas_call(
        pack_kernel,
        out_shape=(pltpu.HBM((devices, capacity0 + META, LANES), bf16),)
        + (pltpu.VMEM((chips, capacity1, LANES), bf16),) * 2,
        in_specs=[ANY, ANY, ANY, VMEM, VMEM, VMEM, VMEM],
        out_specs=(ANY, VMEM, VMEM),
        scratch_shapes=[
            pltpu.VMEM((rows + 2 * EDGE, cols), bf16),
            pltpu.VMEM((rows, cols + 2 * LANES), bf16),
            pltpu.VMEM((pieces, LANES), f32),
            pltpu.VMEM((devices * capacity + 8, LANES), f32),
            pltpu.VMEM((devices, capacity0 + META, LANES), bf16),
            pltpu.SemaphoreType.DMA((3 + pieces // LANES,)),
        ]
        + [pltpu.SMEM((1, 1, LANES), i32)] * (pieces // LANES),
        cost_estimate=cost(10_000_000_000, 4_000_000),
        compiler_params=params(20),
        name="pack",
    )(far(raw), near(above), near(below), near(tv), near(th), near(dest), near(meta))

    most = 8 * devices
    total = pltpu.VMEM((-(-(slots + 3 * GROUP) // most) * most, LANES), f32)
    with jax.named_scope("every"):
        got = lax.all_to_all(everything, axes, split_axis=0, concat_axis=0, tiled=True)
    with jax.named_scope("swap"):
        take = lax.ppermute(give, axes, [(i, i ^ 1) for i in range(devices)])
    joined = pl.pallas_call(
        join_kernel,
        out_shape=(pltpu.VMEM((2 * capacity1, LANES), bf16),) * chips,
        in_specs=[VMEM, VMEM],
        out_specs=(VMEM,) * chips,
        cost_estimate=cost(1_000_000, 1_000_000),
        compiler_params=params(2),
        name="join",
    )(near(keep), near(take))
    rest = [joined[0]]
    with jax.named_scope("rest"):
        for j in range(1, chips):
            rest.append(lax.ppermute(joined[j], axes, [(i, i ^ (2 * j)) for i in range(devices)]))

    used = -(-capacity0 // LANES)
    spots, factors, weight, *sums = pl.pallas_call(
        functools.partial(first_kernel, slots, parts),
        out_shape=(
            pltpu.VMEM((devices * parts, 1, LANES), i32),
            pltpu.VMEM((devices, 1, LANES), f32),
            pltpu.VMEM((slots // LANES, LANES), f32),
        )
        + (total,) * GROUP,
        in_specs=[VMEM],
        out_specs=(VMEM,) * (3 + GROUP),
        scratch_shapes=[
            pltpu.VMEM((devices * capacity0, LANES), f32),
            pltpu.VMEM((devices * used, 1, LANES), i32),
            pltpu.SemaphoreType.DMA((devices * used,)),
        ]
        + [pltpu.SMEM((1, 1, LANES), i32)] * (devices * used),
        cost_estimate=cost(4_000_000_000, 8_000_000),
        compiler_params=params(8),
        name="sum_first",
    )(near(got))
    used = parts - capacity0 // LANES
    image, weight, *_ = pl.pallas_call(
        functools.partial(last_kernel, devices, capacity0, parts),
        out_shape=(pltpu.HBM((slots, LANES), f32), pltpu.HBM((slots // LANES, LANES), f32)) + (total,) * GROUP,
        in_specs=[VMEM] * (chips + 3 + GROUP),
        out_specs=(ANY, ANY) + (VMEM,) * GROUP,
        scratch_shapes=[
            pltpu.VMEM((devices * capacity1, LANES), f32),
            pltpu.VMEM((devices * used, 1, LANES), i32),
            pltpu.VMEM((slots, LANES), f32),
            pltpu.SemaphoreType.DMA((devices * used + 1,)),
        ]
        + [pltpu.SMEM((1, 1, LANES), i32)] * (devices * used),
        input_output_aliases={chips + 3 + k: 2 + k for k in range(GROUP)},
        cost_estimate=cost(4_000_000_000, 8_000_000),
        compiler_params=params(8),
        name="sum_last",
    )(*[near(x) for x in rest], near(spots), near(factors), near(weight), *[near(x) for x in sums])
    return image[None], weight.reshape(1, slots)


def solution(mesh):
    in_specs = (
        P("expo", "fp", None),
        P(),
        P("expo", "fp"),
        P("expo", "fp"),
        P("expo", "fp"),
        P("expo", "fp", None, None),
        P("expo", "fp", None),
    )
    out_specs = (P(("expo", "fp"), None, None), P(("expo", "fp"), None))
    return jax.shard_map(body, mesh=mesh, in_specs=in_specs, out_specs=out_specs, check_vma=False)
```

```python
import functools

import jax
import jax.numpy as jnp
from jax import lax
from jax.experimental import pallas as pl
from jax.experimental.pallas import tpu as pltpu
from jax.sharding import PartitionSpec as P

GAP = 32
EDGE = 32
LANES = 128
META = 8
GROUP = 8


VMEM = pl.BlockSpec(memory_space=pltpu.VMEM)
ANY = pl.BlockSpec(memory_space=pl.ANY)
f32, bf16, i32 = jnp.float32, jnp.bfloat16, jnp.int32


def iota(shape, dim):
    return lax.broadcasted_iota(i32, shape, dim)


def dot_last(a, b):
    return lax.dot_general(a, b, (((1,), (1,)), ((), ())), preferred_element_type=f32)


def near(x):
    return pltpu.with_memory_space_constraint(x, pltpu.VMEM)


def far(x):
    return pltpu.with_memory_space_constraint(x, pltpu.HBM)


def params(mib):
    return pltpu.CompilerParams(vmem_limit_bytes=mib << 20)


def cost(flops, moved):
    return pl.CostEstimate(flops=flops, bytes_accessed=moved, transcendentals=0)


def halo(shard, axis):
    size = lax.axis_size(axis)
    up = [(i, i + 1) for i in range(size - 1)]
    down = [(i + 1, i) for i in range(size - 1)]
    above = lax.ppermute(shard[-EDGE:], axis, up)
    below = lax.ppermute(shard[:EDGE], axis, down)
    return above, below


def route_kernel(capacity, tile_ref, off_ref, gap_ref, var_ref, id_ref, bank_ref, dest_ref, meta_ref, tv_ref, th_ref, line_ref):
    segs, rows = off_ref.shape
    devices = meta_ref.shape[0] // META
    parts = -(-capacity // LANES)
    gap, var, which_bank = gap_ref[...], var_ref[...], id_ref[...]
    bank = bank_ref[...].astype(f32)
    chosen = jnp.where(which_bank == 0, bank[0], 0.0)
    for k in range(1, bank.shape[0]):
        chosen = jnp.where(which_bank == k, bank[k], chosen)
    taps = bank.shape[2]
    half = taps // 2
    lead = -half % 8
    line_ref[...] = jnp.zeros(line_ref.shape, f32)
    line_ref[:, lead : lead + taps] = chosen
    for ref, which, shift in ((tv_ref, 0, EDGE - half), (th_ref, 1, LANES - half)):
        height, width = ref.shape
        wide = jnp.broadcast_to(line_ref[which : which + 1, :width], (height, width))
        ref[...] = pltpu.roll(wide, shift - lead, 1, stride=1, stride_axis=0).astype(bf16)
    line = iota((1, rows), 1)
    kept = jnp.logical_or(line < gap, line >= gap + GAP)
    before = (iota((rows, rows), 0) < iota((rows, rows), 1)).astype(bf16)
    owner = iota((devices, rows), 0)
    owner8 = iota((devices * META, rows), 0) >> 3
    field = iota((META, rows), 0)
    place = iota((LANES, rows), 0)
    base = jnp.zeros((devices, 1), f32)
    packed = jnp.zeros((devices * META, LANES), f32)
    for s in range(segs):
        tile = jnp.where(kept, tile_ref[s], -1)
        hot = (tile == owner).astype(f32)
        prefix = jnp.dot(hot.astype(bf16), before, preferred_element_type=f32)
        rank = jnp.sum(hot * (prefix + base), axis=0, keepdims=True).astype(i32)
        base = base + jnp.sum(hot, axis=1, keepdims=True)
        dest = jnp.where(kept, tile * capacity + rank, devices * capacity)
        for h in range(rows // LANES):
            dest_ref[s * (rows // LANES) + h] = dest[:, h * LANES : (h + 1) * LANES]
        offset = off_ref[s : s + 1, :]
        part = rank >> 7
        value = jnp.where(field == part, (offset >> 6) + 1, 0)
        value = jnp.where(field == part + parts, offset & 63, value).astype(f32)
        spread = jnp.concatenate([value] * devices, axis=0)
        stack = jnp.where(tile == owner8, spread, 0.0).astype(bf16)
        spot = (place == (rank & (LANES - 1))).astype(bf16)
        packed = packed + dot_last(stack, spot)
    first = var.astype(bf16).astype(f32)
    second = (var - first).astype(bf16).astype(f32)
    third = var - first - second
    row = iota((devices * META, LANES), 0) & (META - 1)
    packed = jnp.where(row == 4, first, packed)
    packed = jnp.where(row == 5, second, packed)
    packed = jnp.where(row == 6, third, packed)
    meta_ref[...] = packed.astype(bf16)


def own_index():
    return lax.axis_index("expo") * lax.axis_size("fp") + lax.axis_index("fp")


def pack_kernel(raw_ref, above_ref, below_ref, tv_ref, th_ref, dest_ref, meta_ref, all_ref, keep_ref, give_ref, edged, vert, conv, spread, stage, sems, *tables):
    devices, extended, _ = all_ref.shape
    me = own_index()
    capacity0 = extended - META
    chips, capacity1, _ = keep_ref.shape
    capacity = capacity0 + capacity1
    rows, cols = raw_ref.shape
    copies = [
        pltpu.make_async_copy(above_ref, edged.at[pl.ds(0, EDGE)], sems.at[0]),
        pltpu.make_async_copy(raw_ref, edged.at[pl.ds(EDGE, rows)], sems.at[1]),
        pltpu.make_async_copy(below_ref, edged.at[pl.ds(EDGE + rows, EDGE)], sems.at[2]),
    ]
    for k, table in enumerate(tables):
        copies.append(pltpu.make_async_copy(dest_ref.at[pl.ds(k, 1)], table, sems.at[3 + k]))
    for copy in copies:
        copy.start()
    vert[:, :LANES] = jnp.zeros((rows, LANES), bf16)
    vert[:, LANES + cols :] = jnp.zeros((rows, LANES), bf16)
    stage[:, capacity0:, :] = meta_ref[...].reshape(devices, META, LANES)
    for copy in copies:
        copy.wait()
    wide = 2 * LANES
    tall = rows + 2 * EDGE
    for c in range(cols // wide):
        part = jnp.dot(tv_ref[:, :tall], edged[:, c * wide : (c + 1) * wide], preferred_element_type=f32)
        vert[:, LANES + c * wide : LANES + (c + 1) * wide] = part.astype(bf16)
    for c in range(cols // wide):
        part = dot_last(vert[:, c * wide : c * wide + 2 * wide], th_ref[...])
        conv[2 * c * rows : (2 * c + 1) * rows, :] = part[:, :LANES]
        conv[(2 * c + 1) * rows : (2 * c + 2) * rows, :] = part[:, LANES:]

    def scatter(r, carry):
        for k, table in enumerate(tables):
            spread[pl.ds(table[0, 0, r], 1), :] = conv[pl.ds(r + k * LANES, 1), :]
        return carry

    lax.fori_loop(0, LANES, scatter, 0, unroll=2)

    def emit(k, carry):
        stage[k, :capacity0, :] = spread[pl.ds(pl.multiple_of(k * capacity, 8), capacity0), :].astype(bf16)
        return carry

    share = devices // 4
    copies = []
    for g in range(4):
        lax.fori_loop(g * share, (g + 1) * share, emit, 0)
        block = pl.ds(g * share, share)
        copies.append(pltpu.make_async_copy(stage.at[block], all_ref.at[block], sems.at[g]))
        copies[-1].start()
    for j in range(chips):
        for out, k in ((keep_ref, 2 * j), (give_ref, 2 * j + 1)):
            out[j] = spread[pl.ds(pl.multiple_of((me ^ k) * capacity + capacity0, 8), capacity1), :].astype(bf16)
    for copy in copies:
        copy.wait()


def join_kernel(keep_ref, take_ref, *outs):
    count = keep_ref.shape[1]
    for j, out in enumerate(outs):
        out[:count, :] = keep_ref[j]
        out[count:, :] = take_ref[j]


def add_rows(tables, scaled, sums, turns, count, first):
    member = iota((GROUP, LANES), 0)
    for p in sorted({p for _, p in tables}):
        low, high = max(first, p * LANES), min(first + count, (p + 1) * LANES)
        for turn in range(turns):

            def rank(r, carry):
                places = [tables[turn * GROUP + k, p][0, 0, r] for k in range(GROUP)]
                start = (r + (turn * count + p * LANES - first)) * GROUP
                fresh = scaled[pl.ds(pl.multiple_of(start, GROUP), GROUP), :]
                held = [acc[pl.ds(place, GROUP), :] for acc, place in zip(sums, places)]
                for k in range(GROUP):
                    sums[k][pl.ds(places[k], GROUP), :] = held[k] + jnp.where(member == k, fresh, 0.0)
                return carry

            lax.fori_loop(low - p * LANES, high - p * LANES, rank, 0, unroll=8)


def first_kernel(slots, parts, values_ref, *refs):
    (spots, factors, weight_out), refs = refs[:3], refs[3:]
    sums, (scaled, shifted, sems), refs = refs[:GROUP], refs[GROUP : GROUP + 3], refs[GROUP + 3 :]
    devices, extended, _ = values_ref.shape
    count = extended - META
    used = -(-count // LANES)
    tables = {(n, p): refs[n * used + p] for n in range(devices) for p in range(used)}
    high_id = iota((slots // LANES, LANES), 0)
    low_id = iota((LANES, LANES), 0)
    weight = jnp.zeros((slots // LANES, LANES), f32)
    share = sums[0].shape[0] // devices
    copies = []
    for n in range(devices):
        turn, member = divmod(n, GROUP)
        for acc in sums:
            acc[n * share : (n + 1) * share, :] = jnp.zeros((share, LANES), f32)
        fields = values_ref[n, count:, :].astype(f32)
        factor = fields[4:5, :] + fields[5:6, :] + fields[6:7, :]
        factors[n] = factor
        for p in range(parts):
            high, low = fields[p : p + 1, :], fields[parts + p : parts + p + 1, :]
            slot = jnp.where(high > 0.5, (high - 1.0) * 64.0 + low, float(slots)).astype(i32)
            spots[n * parts + p] = slot
            if p < used:
                shifted[n * used + p] = slot + (GROUP - member)
            high = ((slot >> 7) == high_id).astype(bf16)
            low = ((slot & (LANES - 1)) == low_id).astype(bf16)
            weight = weight + factor * dot_last(high, low)
        scaled[pl.ds(turn * count * GROUP + member, count, stride=GROUP), :] = values_ref[n, :count, :].astype(f32) * factor
    for k, table in enumerate(tables.values()):
        copies.append(pltpu.make_async_copy(shifted.at[pl.ds(k, 1)], table, sems.at[k]))
        copies[-1].start()
    weight_out[...] = weight
    for copy in copies:
        copy.wait()
    add_rows(tables, scaled, sums, devices // GROUP, count, 0)


def last_kernel(devices, first, parts, *refs):
    chips = devices // 2
    pairs, (spots, factors, weight_in), refs = refs[:chips], refs[chips : chips + 3], refs[chips + 3 + GROUP :]
    (image_ref, weight_ref), sums, refs = refs[:2], refs[2 : 2 + GROUP], refs[2 + GROUP :]
    (scaled, shifted, stage, sems), refs = refs[:4], refs[4:]
    count = pairs[0].shape[0] // 2
    slots = stage.shape[0]
    me = own_index()
    begin = first // LANES
    used = parts - begin
    tables = {(n, begin + p): refs[n * used + p] for n in range(devices) for p in range(used)}
    copies = []
    for k, (n, p) in enumerate(tables):
        shifted[k] = spots[(me ^ n) * parts + p] + (GROUP - n % GROUP)
    for k, table in enumerate(tables.values()):
        copies.append(pltpu.make_async_copy(shifted.at[pl.ds(k, 1)], table, sems.at[k]))
        copies[-1].start()
    copies.append(pltpu.make_async_copy(weight_in, weight_ref, sems.at[len(tables)]))
    copies[-1].start()
    for n in range(devices):
        turn, member = divmod(n, GROUP)
        scaled[pl.ds(turn * count * GROUP + member, count, stride=GROUP), :] = pairs[n // 2][n % 2 * count : (n % 2 + 1) * count, :].astype(f32) * factors[me ^ n]
    for copy in copies:
        copy.wait()
    add_rows(tables, scaled, sums, devices // GROUP, count, first)
    weight = weight_in[...]

    def mean(h, total):
        scale = jnp.broadcast_to(jnp.maximum(weight[h : h + 1, :], 1.0), (LANES, LANES)).T
        return total / scale

    merge(sums, stage, mean, image_ref, sems)


def merge(sums, stage, finish, out_ref, sems):
    copies = []
    blocks = stage.shape[0] // LANES
    quarter = blocks // 4
    for h in range(blocks):
        total = [acc[GROUP + h * LANES : GROUP + (h + 1) * LANES, :] for acc in sums]
        while len(total) > 1:
            total = [a + b for a, b in zip(total[::2], total[1::2])] + total[len(total) // 2 * 2 :]
        stage[h * LANES : (h + 1) * LANES, :] = finish(h, total[0])
        if h % quarter == quarter - 1:
            ready = pl.ds((h + 1 - quarter) * LANES, quarter * LANES)
            copies.append(pltpu.make_async_copy(stage.at[ready], out_ref.at[ready], sems.at[h // quarter]))
            copies[-1].start()
    for copy in copies:
        copy.wait()


def body(raw_pixels, kernel_bank, kernel_ids, inv_var, gap_start, warp_tile, warp_offset):
    _, rows, cols = raw_pixels.shape
    segs = cols // LANES
    axes = ("expo", "fp")
    devices = lax.axis_size("expo") * lax.axis_size("fp")
    pieces = rows * segs
    capacity = 2 * pieces // devices
    parts = -(-capacity // LANES)
    slots = pieces
    shape = jax.ShapeDtypeStruct

    raw = raw_pixels[0]
    above, below = halo(raw, "fp")
    tiles = jnp.transpose(warp_tile[0], (1, 2, 0))
    offsets = jnp.transpose(warp_offset[0], (1, 0))
    tall = -(-(rows + 2 * EDGE) // LANES) * LANES
    dest, meta, tv, th = pl.pallas_call(
        functools.partial(route_kernel, capacity),
        out_shape=(
            pltpu.VMEM((pieces // LANES, 1, LANES), i32),
            pltpu.VMEM((devices * META, LANES), bf16),
            pltpu.VMEM((rows, tall), bf16),
            pltpu.VMEM((2 * LANES, 4 * LANES), bf16),
        ),
        in_specs=[VMEM] * 6,
        out_specs=(VMEM,) * 4,
        scratch_shapes=[pltpu.VMEM((2, 4 * LANES), f32)],
        cost_estimate=cost(400_000_000, 600_000),
        compiler_params=params(16),
        name="route",
    )(far(tiles), far(offsets), gap_start, inv_var, kernel_ids, far(kernel_bank))

    capacity1 = capacity * 5 // 16 // 8 * 8
    capacity0 = capacity - capacity1
    chips = devices // 2
    everything, keep, give = pl.pallas_call(
        pack_kernel,
        out_shape=(pltpu.HBM((devices, capacity0 + META, LANES), bf16),)
        + (pltpu.VMEM((chips, capacity1, LANES), bf16),) * 2,
        in_specs=[ANY, ANY, ANY, VMEM, VMEM, VMEM, VMEM],
        out_specs=(ANY, VMEM, VMEM),
        scratch_shapes=[
            pltpu.VMEM((rows + 2 * EDGE, cols), bf16),
            pltpu.VMEM((rows, cols + 2 * LANES), bf16),
            pltpu.VMEM((pieces, LANES), f32),
            pltpu.VMEM((devices * capacity + 8, LANES), f32),
            pltpu.VMEM((devices, capacity0 + META, LANES), bf16),
            pltpu.SemaphoreType.DMA((3 + pieces // LANES,)),
        ]
        + [pltpu.SMEM((1, 1, LANES), i32)] * (pieces // LANES),
        cost_estimate=cost(10_000_000_000, 4_000_000),
        compiler_params=params(20),
        name="pack",
    )(far(raw), near(above), near(below), near(tv), near(th), near(dest), near(meta))

    most = 8 * devices
    total = pltpu.VMEM((-(-(slots + 3 * GROUP) // most) * most, LANES), f32)
    with jax.named_scope("every"):
        got = lax.all_to_all(everything, axes, split_axis=0, concat_axis=0, tiled=True)
    with jax.named_scope("swap"):
        take = lax.ppermute(give, axes, [(i, i ^ 1) for i in range(devices)])
    joined = pl.pallas_call(
        join_kernel,
        out_shape=(pltpu.VMEM((2 * capacity1, LANES), bf16),) * chips,
        in_specs=[VMEM, VMEM],
        out_specs=(VMEM,) * chips,
        cost_estimate=cost(1_000_000, 1_000_000),
        compiler_params=params(2),
        name="join",
    )(near(keep), near(take))
    rest = [joined[0]] * chips
    with jax.named_scope("rest"):
        for j in sorted(range(1, chips), key=lambda j: (bin(j & 3).count("1") + (j & 3 > 1), j)):
            rest[j] = lax.ppermute(joined[j], axes, [(i, i ^ (2 * j)) for i in range(devices)])

    used = -(-capacity0 // LANES)
    spots, factors, weight, *sums = pl.pallas_call(
        functools.partial(first_kernel, slots, parts),
        out_shape=(
            pltpu.VMEM((devices * parts, 1, LANES), i32),
            pltpu.VMEM((devices, 1, LANES), f32),
            pltpu.VMEM((slots // LANES, LANES), f32),
        )
        + (total,) * GROUP,
        in_specs=[VMEM],
        out_specs=(VMEM,) * (3 + GROUP),
        scratch_shapes=[
            pltpu.VMEM((devices * capacity0, LANES), f32),
            pltpu.VMEM((devices * used, 1, LANES), i32),
            pltpu.SemaphoreType.DMA((devices * used,)),
        ]
        + [pltpu.SMEM((1, 1, LANES), i32)] * (devices * used),
        cost_estimate=cost(4_000_000_000, 8_000_000),
        compiler_params=params(8),
        name="sum_first",
    )(near(got))
    used = parts - capacity0 // LANES
    image, weight, *_ = pl.pallas_call(
        functools.partial(last_kernel, devices, capacity0, parts),
        out_shape=(pltpu.HBM((slots, LANES), f32), pltpu.HBM((slots // LANES, LANES), f32)) + (total,) * GROUP,
        in_specs=[VMEM] * (chips + 3 + GROUP),
        out_specs=(ANY, ANY) + (VMEM,) * GROUP,
        scratch_shapes=[
            pltpu.VMEM((devices * capacity1, LANES), f32),
            pltpu.VMEM((devices * used, 1, LANES), i32),
            pltpu.VMEM((slots, LANES), f32),
            pltpu.SemaphoreType.DMA((devices * used + 1,)),
        ]
        + [pltpu.SMEM((1, 1, LANES), i32)] * (devices * used),
        input_output_aliases={chips + 3 + k: 2 + k for k in range(GROUP)},
        cost_estimate=cost(4_000_000_000, 8_000_000),
        compiler_params=params(8),
        name="sum_last",
    )(*[near(x) for x in rest], near(spots), near(factors), near(weight), *[near(x) for x in sums])
    return image[None], weight.reshape(1, slots)


def solution(mesh):
    in_specs = (
        P("expo", "fp", None),
        P(),
        P("expo", "fp"),
        P("expo", "fp"),
        P("expo", "fp"),
        P("expo", "fp", None, None),
        P("expo", "fp", None),
    )
    out_specs = (P(("expo", "fp"), None, None), P(("expo", "fp"), None))
    return jax.shard_map(body, mesh=mesh, in_specs=in_specs, out_specs=out_specs, check_vma=False)
```

```python
import functools

import jax
import jax.numpy as jnp
from jax import lax
from jax.experimental import pallas as pl
from jax.experimental.pallas import tpu as pltpu
from jax.sharding import PartitionSpec as P


GAP = 32
EDGE = 32
LANES = 128
META = 8
GROUP = 8


VMEM = pl.BlockSpec(memory_space=pltpu.VMEM)
ANY = pl.BlockSpec(memory_space=pl.ANY)
f32, bf16, i32 = jnp.float32, jnp.bfloat16, jnp.int32


def iota(shape, dim):
    return lax.broadcasted_iota(i32, shape, dim)


def dot_last(a, b):
    return lax.dot_general(a, b, (((1,), (1,)), ((), ())), preferred_element_type=f32)


def near(x):
    return pltpu.with_memory_space_constraint(x, pltpu.VMEM)


def far(x):
    return pltpu.with_memory_space_constraint(x, pltpu.HBM)


def params(mib):
    return pltpu.CompilerParams(vmem_limit_bytes=mib << 20)


def cost(flops, moved):
    return pl.CostEstimate(flops=flops, bytes_accessed=moved, transcendentals=0)


def halo(shard, axis):
    size = lax.axis_size(axis)
    up = [(i, i + 1) for i in range(size - 1)]
    down = [(i + 1, i) for i in range(size - 1)]
    above = lax.ppermute(shard[-EDGE:], axis, up)
    below = lax.ppermute(shard[:EDGE], axis, down)
    return above, below


def route_kernel(capacity, tile_ref, off_ref, gap_ref, var_ref, id_ref, bank_ref, dest_ref, meta_ref, tv_ref, th_ref, line_ref):
    segs, rows = off_ref.shape
    devices = meta_ref.shape[0] // META
    parts = -(-capacity // LANES)
    gap, var, which_bank = gap_ref[...], var_ref[...], id_ref[...]
    bank = bank_ref[...].astype(f32)
    chosen = jnp.where(which_bank == 0, bank[0], 0.0)
    for k in range(1, bank.shape[0]):
        chosen = jnp.where(which_bank == k, bank[k], chosen)
    taps = bank.shape[2]
    half = taps // 2
    lead = -half % 8
    line_ref[...] = jnp.zeros(line_ref.shape, f32)
    line_ref[:, lead : lead + taps] = chosen
    for ref, which, shift in ((tv_ref, 0, EDGE - half), (th_ref, 1, LANES - half)):
        height, width = ref.shape
        wide = jnp.broadcast_to(line_ref[which : which + 1, :width], (height, width))
        ref[...] = pltpu.roll(wide, shift - lead, 1, stride=1, stride_axis=0).astype(bf16)
    line = iota((1, rows), 1)
    kept = jnp.logical_or(line < gap, line >= gap + GAP)
    before = (iota((rows, rows), 0) < iota((rows, rows), 1)).astype(bf16)
    owner = iota((devices, rows), 0)
    owner8 = iota((devices * META, rows), 0) >> 3
    field = iota((META, rows), 0)
    place = iota((LANES, rows), 0)
    base = jnp.zeros((devices, 1), f32)
    packed = jnp.zeros((devices * META, LANES), f32)
    for s in range(segs):
        tile = jnp.where(kept, tile_ref[s], -1)
        hot = (tile == owner).astype(f32)
        prefix = jnp.dot(hot.astype(bf16), before, preferred_element_type=f32)
        rank = jnp.sum(hot * (prefix + base), axis=0, keepdims=True).astype(i32)
        base = base + jnp.sum(hot, axis=1, keepdims=True)
        dest = jnp.where(kept, tile * capacity + rank, devices * capacity)
        for h in range(rows // LANES):
            dest_ref[s * (rows // LANES) + h] = dest[:, h * LANES : (h + 1) * LANES]
        offset = off_ref[s : s + 1, :]
        part = rank >> 7
        value = jnp.where(field == part, (offset >> 6) + 1, 0)
        value = jnp.where(field == part + parts, offset & 63, value).astype(f32)
        spread = jnp.concatenate([value] * devices, axis=0)
        stack = jnp.where(tile == owner8, spread, 0.0).astype(bf16)
        spot = (place == (rank & (LANES - 1))).astype(bf16)
        packed = packed + dot_last(stack, spot)
    first = var.astype(bf16).astype(f32)
    second = (var - first).astype(bf16).astype(f32)
    third = var - first - second
    row = iota((devices * META, LANES), 0) & (META - 1)
    packed = jnp.where(row == 4, first, packed)
    packed = jnp.where(row == 5, second, packed)
    packed = jnp.where(row == 6, third, packed)
    meta_ref[...] = packed.astype(bf16)


def own_index():
    return lax.axis_index("expo") * lax.axis_size("fp") + lax.axis_index("fp")


def pack_kernel(raw_ref, above_ref, below_ref, tv_ref, th_ref, dest_ref, meta_ref, all_ref, keep_ref, give_ref, edged, vert, conv, spread, stage, sems, *tables):
    devices, extended, _ = all_ref.shape
    me = own_index()
    capacity0 = extended - META
    chips, capacity1, _ = keep_ref.shape
    capacity = capacity0 + capacity1
    rows, cols = raw_ref.shape
    copies = [
        pltpu.make_async_copy(above_ref, edged.at[pl.ds(0, EDGE)], sems.at[0]),
        pltpu.make_async_copy(raw_ref, edged.at[pl.ds(EDGE, rows)], sems.at[1]),
        pltpu.make_async_copy(below_ref, edged.at[pl.ds(EDGE + rows, EDGE)], sems.at[2]),
    ]
    for k, table in enumerate(tables):
        copies.append(pltpu.make_async_copy(dest_ref.at[pl.ds(k, 1)], table, sems.at[3 + k]))
    for copy in copies:
        copy.start()
    vert[:, :LANES] = jnp.zeros((rows, LANES), bf16)
    vert[:, LANES + cols :] = jnp.zeros((rows, LANES), bf16)
    stage[:, capacity0:, :] = meta_ref[...].reshape(devices, META, LANES)
    for copy in copies:
        copy.wait()
    wide = 2 * LANES
    tall = rows + 2 * EDGE
    for c in range(cols // wide):
        part = jnp.dot(tv_ref[:, :tall], edged[:, c * wide : (c + 1) * wide], preferred_element_type=f32)
        vert[:, LANES + c * wide : LANES + (c + 1) * wide] = part.astype(bf16)
    for c in range(cols // wide):
        part = dot_last(vert[:, c * wide : c * wide + 2 * wide], th_ref[...])
        conv[2 * c * rows : (2 * c + 1) * rows, :] = part[:, :LANES]
        conv[(2 * c + 1) * rows : (2 * c + 2) * rows, :] = part[:, LANES:]

    def scatter(r, carry):
        for k, table in enumerate(tables):
            spread[pl.ds(table[0, 0, r], 1), :] = conv[pl.ds(r + k * LANES, 1), :]
        return carry

    lax.fori_loop(0, LANES, scatter, 0, unroll=2)

    def emit(k, carry):
        stage[k, :capacity0, :] = spread[pl.ds(pl.multiple_of(k * capacity, 8), capacity0), :].astype(bf16)
        return carry

    share = devices // 4
    copies = []
    for g in range(4):
        lax.fori_loop(g * share, (g + 1) * share, emit, 0)
        block = pl.ds(g * share, share)
        copies.append(pltpu.make_async_copy(stage.at[block], all_ref.at[block], sems.at[g]))
        copies[-1].start()
    for j in range(chips):
        for out, k in ((keep_ref, 2 * j), (give_ref, 2 * j + 1)):
            out[j] = spread[pl.ds(pl.multiple_of((me ^ k) * capacity + capacity0, 8), capacity1), :].astype(bf16)
    for copy in copies:
        copy.wait()


def join_kernel(keep_ref, take_ref, *outs):
    count = keep_ref.shape[1]
    for j, out in enumerate(outs):
        out[:count, :] = keep_ref[j]
        out[count:, :] = take_ref[j]


def add_rows(tables, scaled, sums, turns, count, first):
    member = iota((GROUP, LANES), 0)
    for p in sorted({p for _, p in tables}):
        low, high = max(first, p * LANES), min(first + count, (p + 1) * LANES)
        for turn in range(turns):

            def rank(r, carry):
                places = [tables[turn * GROUP + k, p][0, 0, r] for k in range(GROUP)]
                start = (r + (turn * count + p * LANES - first)) * GROUP
                fresh = scaled[pl.ds(pl.multiple_of(start, GROUP), GROUP), :]
                held = [acc[pl.ds(place, GROUP), :] for acc, place in zip(sums, places)]
                for k in range(GROUP):
                    sums[k][pl.ds(places[k], GROUP), :] = held[k] + jnp.where(member == k, fresh, 0.0)
                return carry

            lax.fori_loop(low - p * LANES, high - p * LANES, rank, 0, unroll=8)


def first_kernel(slots, parts, values_ref, *refs):
    (spots, factors, weight_out), refs = refs[:3], refs[3:]
    sums, (scaled, shifted, sems), refs = refs[:GROUP], refs[GROUP : GROUP + 3], refs[GROUP + 3 :]
    devices, extended, _ = values_ref.shape
    count = extended - META
    used = -(-count // LANES)
    tables = {(n, p): refs[n * used + p] for n in range(devices) for p in range(used)}
    high_id = iota((slots // LANES, LANES), 0)
    low_id = iota((LANES, LANES), 0)
    weight = jnp.zeros((slots // LANES, LANES), f32)
    share = sums[0].shape[0] // devices
    copies = []
    for n in range(devices):
        turn, member = divmod(n, GROUP)
        for acc in sums:
            acc[n * share : (n + 1) * share, :] = jnp.zeros((share, LANES), f32)
        fields = values_ref[n, count:, :].astype(f32)
        factor = fields[4:5, :] + fields[5:6, :] + fields[6:7, :]
        factors[n] = factor
        for p in range(parts):
            high, low = fields[p : p + 1, :], fields[parts + p : parts + p + 1, :]
            slot = jnp.where(high > 0.5, (high - 1.0) * 64.0 + low, float(slots)).astype(i32)
            spots[n * parts + p] = slot
            if p < used:
                shifted[n * used + p] = slot + (GROUP - member)
            high = ((slot >> 7) == high_id).astype(bf16)
            low = ((slot & (LANES - 1)) == low_id).astype(bf16)
            weight = weight + factor * dot_last(high, low)
        scaled[pl.ds(turn * count * GROUP + member, count, stride=GROUP), :] = values_ref[n, :count, :].astype(f32) * factor
    for k, table in enumerate(tables.values()):
        copies.append(pltpu.make_async_copy(shifted.at[pl.ds(k, 1)], table, sems.at[k]))
        copies[-1].start()
    weight_out[...] = weight
    for copy in copies:
        copy.wait()
    add_rows(tables, scaled, sums, devices // GROUP, count, 0)


def rest_kernel(low, high, first, parts, closes, *refs):
    chips = high - low
    pairs, (spots, factors), refs = refs[:chips], refs[chips : chips + 2], refs[chips + 2 :]
    weight_in, refs = (refs[0], refs[1:]) if closes else (None, refs)
    refs = refs[GROUP:]
    (image_ref, weight_ref), refs = (refs[:2], refs[2:]) if closes else ((None, None), refs)
    sums, (scaled, shifted, sems), refs = refs[:GROUP], refs[GROUP : GROUP + 3], refs[GROUP + 3 :]
    stage, refs = (refs[0], refs[1:]) if closes else (None, refs)
    count = pairs[0].shape[0] // 2
    me = own_index()
    begin = first // LANES
    used = parts - begin
    sources = 2 * chips
    tables = {(n, begin + p): refs[n * used + p] for n in range(sources) for p in range(used)}
    copies = []
    if closes:
        copies.append(pltpu.make_async_copy(weight_in, weight_ref, sems.at[len(tables)]))
        copies[0].start()
    for k, (n, p) in enumerate(tables):
        shifted[k] = spots[(me ^ (2 * low + n)) * parts + p] + (GROUP - n % GROUP)
    for k, table in enumerate(tables.values()):
        copies.append(pltpu.make_async_copy(shifted.at[pl.ds(k, 1)], table, sems.at[k]))
        copies[-1].start()
    for n in range(sources):
        turn, member = divmod(n, GROUP)
        rows = pairs[n // 2][n % 2 * count : (n % 2 + 1) * count, :].astype(f32)
        scaled[pl.ds(turn * count * GROUP + member, count, stride=GROUP), :] = rows * factors[me ^ (2 * low + n)]
    for copy in copies:
        copy.wait()
    add_rows(tables, scaled, sums, sources // GROUP, count, first)
    if not closes:
        return
    weight = weight_in[...]

    def mean(h, total):
        scale = jnp.broadcast_to(jnp.maximum(weight[h : h + 1, :], 1.0), (LANES, LANES)).T
        return total / scale

    merge(sums, stage, mean, image_ref, sems)


def merge(sums, stage, finish, out_ref, sems):
    copies = []
    blocks = stage.shape[0] // LANES
    quarter = blocks // 4
    for h in range(blocks):
        total = [acc[GROUP + h * LANES : GROUP + (h + 1) * LANES, :] for acc in sums]
        while len(total) > 1:
            total = [a + b for a, b in zip(total[::2], total[1::2])] + total[len(total) // 2 * 2 :]
        stage[h * LANES : (h + 1) * LANES, :] = finish(h, total[0])
        if h % quarter == quarter - 1:
            ready = pl.ds((h + 1 - quarter) * LANES, quarter * LANES)
            copies.append(pltpu.make_async_copy(stage.at[ready], out_ref.at[ready], sems.at[h // quarter]))
            copies[-1].start()
    for copy in copies:
        copy.wait()


def body(raw_pixels, kernel_bank, kernel_ids, inv_var, gap_start, warp_tile, warp_offset):
    _, rows, cols = raw_pixels.shape
    segs = cols // LANES
    axes = ("expo", "fp")
    devices = lax.axis_size("expo") * lax.axis_size("fp")
    pieces = rows * segs
    capacity = 2 * pieces // devices
    parts = -(-capacity // LANES)
    slots = pieces

    raw = raw_pixels[0]
    above, below = halo(raw, "fp")
    tiles = jnp.transpose(warp_tile[0], (1, 2, 0))
    offsets = jnp.transpose(warp_offset[0], (1, 0))
    tall = -(-(rows + 2 * EDGE) // LANES) * LANES
    dest, meta, tv, th = pl.pallas_call(
        functools.partial(route_kernel, capacity),
        out_shape=(
            pltpu.VMEM((pieces // LANES, 1, LANES), i32),
            pltpu.VMEM((devices * META, LANES), bf16),
            pltpu.VMEM((rows, tall), bf16),
            pltpu.VMEM((2 * LANES, 4 * LANES), bf16),
        ),
        in_specs=[VMEM] * 6,
        out_specs=(VMEM,) * 4,
        scratch_shapes=[pltpu.VMEM((2, 4 * LANES), f32)],
        cost_estimate=cost(400_000_000, 600_000),
        compiler_params=params(16),
        name="route",
    )(far(tiles), far(offsets), gap_start, inv_var, kernel_ids, far(kernel_bank))

    capacity1 = capacity // 2
    capacity0 = capacity - capacity1
    chips = devices // 2
    everything, keep, give = pl.pallas_call(
        pack_kernel,
        out_shape=(pltpu.HBM((devices, capacity0 + META, LANES), bf16),)
        + (pltpu.VMEM((chips, capacity1, LANES), bf16),) * 2,
        in_specs=[ANY, ANY, ANY, VMEM, VMEM, VMEM, VMEM],
        out_specs=(ANY, VMEM, VMEM),
        scratch_shapes=[
            pltpu.VMEM((rows + 2 * EDGE, cols), bf16),
            pltpu.VMEM((rows, cols + 2 * LANES), bf16),
            pltpu.VMEM((pieces, LANES), f32),
            pltpu.VMEM((devices * capacity + 8, LANES), f32),
            pltpu.VMEM((devices, capacity0 + META, LANES), bf16),
            pltpu.SemaphoreType.DMA((3 + pieces // LANES,)),
        ]
        + [pltpu.SMEM((1, 1, LANES), i32)] * (pieces // LANES),
        cost_estimate=cost(10_000_000_000, 4_000_000),
        compiler_params=params(20),
        name="pack",
    )(far(raw), near(above), near(below), near(tv), near(th), near(dest), near(meta))

    most = 8 * devices
    total = pltpu.VMEM((-(-(slots + 3 * GROUP) // most) * most, LANES), f32)
    got = lax.all_to_all(everything, axes, split_axis=0, concat_axis=0, tiled=True)
    take = lax.ppermute(give, axes, [(i, i ^ 1) for i in range(devices)])
    joined = pl.pallas_call(
        join_kernel,
        out_shape=(pltpu.VMEM((2 * capacity1, LANES), bf16),) * chips,
        in_specs=[VMEM, VMEM],
        out_specs=(VMEM,) * chips,
        cost_estimate=cost(1_000_000, 1_000_000),
        compiler_params=params(2),
        name="join",
    )(near(keep), near(take))
    rest = [joined[0]]
    cuts = (0, chips // 2, chips * 3 // 4, chips)
    for low, high in zip(cuts, cuts[1:]):
        for j in range(max(low, 1), high):
            rest.append(lax.ppermute(joined[j], axes, [(i, i ^ (2 * j)) for i in range(devices)]))

    used = -(-capacity0 // LANES)
    spots, factors, weight, *sums = pl.pallas_call(
        functools.partial(first_kernel, slots, parts),
        out_shape=(
            pltpu.VMEM((devices * parts, 1, LANES), i32),
            pltpu.VMEM((devices, 1, LANES), f32),
            pltpu.VMEM((slots // LANES, LANES), f32),
        )
        + (total,) * GROUP,
        in_specs=[VMEM],
        out_specs=(VMEM,) * (3 + GROUP),
        scratch_shapes=[
            pltpu.VMEM((devices * capacity0, LANES), f32),
            pltpu.VMEM((devices * used, 1, LANES), i32),
            pltpu.SemaphoreType.DMA((devices * used,)),
        ]
        + [pltpu.SMEM((1, 1, LANES), i32)] * (devices * used),
        cost_estimate=cost(4_000_000_000, 8_000_000),
        compiler_params=params(8),
        name="sum_first",
    )(near(got))
    used = parts - capacity0 // LANES
    for low, high in zip(cuts, cuts[1:]):
        closes = high == chips
        number, here = high - low, 2 * (high - low)
        ends = (pltpu.HBM((slots, LANES), f32), pltpu.HBM((slots // LANES, LANES), f32)) if closes else ()
        lead = number + 2 + closes
        out = pl.pallas_call(
            functools.partial(rest_kernel, low, high, capacity0, parts, closes),
            out_shape=ends + (total,) * GROUP,
            in_specs=[VMEM] * (lead + GROUP),
            out_specs=(ANY,) * len(ends) + (VMEM,) * GROUP,
            scratch_shapes=[
                pltpu.VMEM((here * capacity1, LANES), f32),
                pltpu.VMEM((here * used, 1, LANES), i32),
                pltpu.SemaphoreType.DMA((here * used + 1,)),
            ]
            + [pltpu.VMEM((slots, LANES), f32)] * closes
            + [pltpu.SMEM((1, 1, LANES), i32)] * (here * used),
            input_output_aliases={lead + k: len(ends) + k for k in range(GROUP)},
            cost_estimate=cost(4_000_000_000, 8_000_000),
            compiler_params=params(8),
        )(
            *[near(x) for x in rest[low:high]],
            near(spots),
            near(factors),
            *[near(weight)] * closes,
            *[near(x) for x in sums],
        )
        sums = out[len(ends) :]
    image, weight = out[:2]
    return image[None], weight.reshape(1, slots)


def solution(mesh):
    in_specs = (
        P("expo", "fp", None),
        P(),
        P("expo", "fp"),
        P("expo", "fp"),
        P("expo", "fp"),
        P("expo", "fp", None, None),
        P("expo", "fp", None),
    )
    out_specs = (P(("expo", "fp"), None, None), P(("expo", "fp"), None))
    return jax.shard_map(body, mesh=mesh, in_specs=in_specs, out_specs=out_specs, check_vma=False)
```

```python
import functools

import jax
import jax.numpy as jnp
from jax import lax
from jax.experimental import pallas as pl
from jax.experimental.pallas import tpu as pltpu
from jax.sharding import PartitionSpec as P


GAP = 32
EDGE = 32
LANES = 128
META = 8
GROUP = 8


VMEM = pl.BlockSpec(memory_space=pltpu.VMEM)
ANY = pl.BlockSpec(memory_space=pl.ANY)
f32, bf16, i32 = jnp.float32, jnp.bfloat16, jnp.int32


def iota(shape, dim):
    return lax.broadcasted_iota(i32, shape, dim)


def dot_last(a, b):
    return lax.dot_general(a, b, (((1,), (1,)), ((), ())), preferred_element_type=f32)


def near(x):
    return pltpu.with_memory_space_constraint(x, pltpu.VMEM)


def far(x):
    return pltpu.with_memory_space_constraint(x, pltpu.HBM)


def params(mib):
    return pltpu.CompilerParams(vmem_limit_bytes=mib << 20)


def cost(flops, moved):
    return pl.CostEstimate(flops=flops, bytes_accessed=moved, transcendentals=0)


def halo(shard, axis):
    size = lax.axis_size(axis)
    up = [(i, i + 1) for i in range(size - 1)]
    down = [(i + 1, i) for i in range(size - 1)]
    above = lax.ppermute(shard[-EDGE:], axis, up)
    below = lax.ppermute(shard[:EDGE], axis, down)
    return above, below


def route_kernel(capacity, tile_ref, off_ref, gap_ref, var_ref, id_ref, bank_ref, dest_ref, meta_ref, tv_ref, th_ref, line_ref):
    segs, rows = off_ref.shape
    devices = meta_ref.shape[0] // META
    parts = -(-capacity // LANES)
    gap, var, which_bank = gap_ref[...], var_ref[...], id_ref[...]
    bank = bank_ref[...].astype(f32)
    chosen = jnp.where(which_bank == 0, bank[0], 0.0)
    for k in range(1, bank.shape[0]):
        chosen = jnp.where(which_bank == k, bank[k], chosen)
    taps = bank.shape[2]
    half = taps // 2
    lead = -half % 8
    line_ref[...] = jnp.zeros(line_ref.shape, f32)
    line_ref[:, lead : lead + taps] = chosen
    for ref, which, shift in ((tv_ref, 0, EDGE - half), (th_ref, 1, LANES - half)):
        height, width = ref.shape
        wide = jnp.broadcast_to(line_ref[which : which + 1, :width], (height, width))
        ref[...] = pltpu.roll(wide, shift - lead, 1, stride=1, stride_axis=0).astype(bf16)
    line = iota((1, rows), 1)
    kept = jnp.logical_or(line < gap, line >= gap + GAP)
    before = (iota((rows, rows), 0) < iota((rows, rows), 1)).astype(bf16)
    owner = iota((devices, rows), 0)
    owner8 = iota((devices * META, rows), 0) >> 3
    field = iota((META, rows), 0)
    place = iota((LANES, rows), 0)
    base = jnp.zeros((devices, 1), f32)
    packed = jnp.zeros((devices * META, LANES), f32)
    for s in range(segs):
        tile = jnp.where(kept, tile_ref[s], -1)
        hot = (tile == owner).astype(f32)
        prefix = jnp.dot(hot.astype(bf16), before, preferred_element_type=f32)
        rank = jnp.sum(hot * (prefix + base), axis=0, keepdims=True).astype(i32)
        base = base + jnp.sum(hot, axis=1, keepdims=True)
        dest = jnp.where(kept, tile * capacity + rank, devices * capacity)
        for h in range(rows // LANES):
            dest_ref[s * (rows // LANES) + h] = dest[:, h * LANES : (h + 1) * LANES]
        offset = off_ref[s : s + 1, :]
        part = rank >> 7
        value = jnp.where(field == part, (offset >> 6) + 1, 0)
        value = jnp.where(field == part + parts, offset & 63, value).astype(f32)
        spread = jnp.concatenate([value] * devices, axis=0)
        stack = jnp.where(tile == owner8, spread, 0.0).astype(bf16)
        spot = (place == (rank & (LANES - 1))).astype(bf16)
        packed = packed + dot_last(stack, spot)
    first = var.astype(bf16).astype(f32)
    second = (var - first).astype(bf16).astype(f32)
    third = var - first - second
    row = iota((devices * META, LANES), 0) & (META - 1)
    packed = jnp.where(row == 4, first, packed)
    packed = jnp.where(row == 5, second, packed)
    packed = jnp.where(row == 6, third, packed)
    meta_ref[...] = packed.astype(bf16)


def own_index():
    return lax.axis_index("expo") * lax.axis_size("fp") + lax.axis_index("fp")


def pack_kernel(raw_ref, above_ref, below_ref, tv_ref, th_ref, dest_ref, meta_ref, all_ref, keep_ref, give_ref, edged, vert, conv, spread, stage, sems, *tables):
    devices, extended, _ = all_ref.shape
    me = own_index()
    capacity0 = extended - META
    chips, capacity1, _ = keep_ref.shape
    capacity = capacity0 + capacity1
    rows, cols = raw_ref.shape
    copies = [
        pltpu.make_async_copy(above_ref, edged.at[pl.ds(0, EDGE)], sems.at[0]),
        pltpu.make_async_copy(raw_ref, edged.at[pl.ds(EDGE, rows)], sems.at[1]),
        pltpu.make_async_copy(below_ref, edged.at[pl.ds(EDGE + rows, EDGE)], sems.at[2]),
    ]
    for k, table in enumerate(tables):
        copies.append(pltpu.make_async_copy(dest_ref.at[pl.ds(k, 1)], table, sems.at[3 + k]))
    for copy in copies:
        copy.start()
    vert[:, :LANES] = jnp.zeros((rows, LANES), bf16)
    vert[:, LANES + cols :] = jnp.zeros((rows, LANES), bf16)
    stage[:, capacity0:, :] = meta_ref[...].reshape(devices, META, LANES)
    for copy in copies:
        copy.wait()
    wide = 2 * LANES
    tall = rows + 2 * EDGE
    blocks = cols // wide
    turn = rows // LANES

    def vertical(c):
        part = jnp.dot(tv_ref[:, :tall], edged[:, c * wide : (c + 1) * wide], preferred_element_type=f32)
        vert[:, LANES + c * wide : LANES + (c + 1) * wide] = part.astype(bf16)

    def horizontal(c):
        part = dot_last(vert[:, c * wide : c * wide + 2 * wide], th_ref[...])
        conv[2 * c * rows : (2 * c + 1) * rows, :] = part[:, :LANES]
        conv[(2 * c + 1) * rows : (2 * c + 2) * rows, :] = part[:, LANES:]

    vertical(0)
    vertical(1)
    horizontal(0)
    for c in range(blocks):
        if c + 2 < blocks:
            vertical(c + 2)
        if c + 1 < blocks:
            horizontal(c + 1)
        for k in range(2 * c * turn, 2 * (c + 1) * turn):
            for r in range(LANES):
                spread[pl.ds(tables[k][0, 0, r], 1), :] = conv[k * LANES + r : k * LANES + r + 1, :]

    def emit(k, carry):
        stage[k, :capacity0, :] = spread[pl.ds(pl.multiple_of(k * capacity, 8), capacity0), :].astype(bf16)
        return carry

    share = devices // 4
    copies = []
    for g in range(4):
        lax.fori_loop(g * share, (g + 1) * share, emit, 0)
        block = pl.ds(g * share, share)
        copies.append(pltpu.make_async_copy(stage.at[block], all_ref.at[block], sems.at[g]))
        copies[-1].start()
    for j in range(chips):
        for out, k in ((keep_ref, 2 * j), (give_ref, 2 * j + 1)):
            out[j] = spread[pl.ds(pl.multiple_of((me ^ k) * capacity + capacity0, 8), capacity1), :].astype(bf16)
    for copy in copies:
        copy.wait()


def join_kernel(keep_ref, take_ref, *outs):
    count = keep_ref.shape[1]
    for j, out in enumerate(outs):
        out[:count, :] = keep_ref[j]
        out[count:, :] = take_ref[j]


def add_rows(tables, scaled, sums, turns, count, first):
    member = iota((GROUP, LANES), 0)
    for p in sorted({p for _, p in tables}):
        low, high = max(first, p * LANES), min(first + count, (p + 1) * LANES)
        for turn in range(turns):

            def rank(r, carry):
                places = [tables[turn * GROUP + k, p][0, 0, r] for k in range(GROUP)]
                start = (r + (turn * count + p * LANES - first)) * GROUP
                fresh = scaled[pl.ds(pl.multiple_of(start, GROUP), GROUP), :]
                held = [acc[pl.ds(place, GROUP), :] for acc, place in zip(sums, places)]
                for k in range(GROUP):
                    sums[k][pl.ds(places[k], GROUP), :] = held[k] + jnp.where(member == k, fresh, 0.0)
                return carry

            lax.fori_loop(low - p * LANES, high - p * LANES, rank, 0, unroll=8)


def first_kernel(slots, parts, values_ref, *refs):
    (spots, factors, weight_out), refs = refs[:3], refs[3:]
    sums, (scaled, shifted, sems), refs = refs[:GROUP], refs[GROUP : GROUP + 3], refs[GROUP + 3 :]
    devices, extended, _ = values_ref.shape
    count = extended - META
    used = -(-count // LANES)
    tables = {(n, p): refs[n * used + p] for n in range(devices) for p in range(used)}
    high_id = iota((slots // LANES, LANES), 0)
    low_id = iota((LANES, LANES), 0)
    weight = jnp.zeros((slots // LANES, LANES), f32)
    share = sums[0].shape[0] // devices
    copies = []
    for n in range(devices):
        turn, member = divmod(n, GROUP)
        for acc in sums:
            acc[n * share : (n + 1) * share, :] = jnp.zeros((share, LANES), f32)
        fields = values_ref[n, count:, :].astype(f32)
        factor = fields[4:5, :] + fields[5:6, :] + fields[6:7, :]
        factors[n] = factor
        for p in range(parts):
            high, low = fields[p : p + 1, :], fields[parts + p : parts + p + 1, :]
            slot = jnp.where(high > 0.5, (high - 1.0) * 64.0 + low, float(slots)).astype(i32)
            spots[n * parts + p] = slot
            if p < used:
                shifted[n * used + p] = slot + (GROUP - member)
            high = ((slot >> 7) == high_id).astype(bf16)
            low = ((slot & (LANES - 1)) == low_id).astype(bf16)
            weight = weight + factor * dot_last(high, low)
        scaled[pl.ds(turn * count * GROUP + member, count, stride=GROUP), :] = values_ref[n, :count, :].astype(f32) * factor
    for k, table in enumerate(tables.values()):
        copies.append(pltpu.make_async_copy(shifted.at[pl.ds(k, 1)], table, sems.at[k]))
        copies[-1].start()
    weight_out[...] = weight
    for copy in copies:
        copy.wait()
    add_rows(tables, scaled, sums, devices // GROUP, count, 0)


def rest_kernel(low, high, first, parts, closes, *refs):
    chips = high - low
    pairs, (spots, factors), refs = refs[:chips], refs[chips : chips + 2], refs[chips + 2 :]
    weight_in, refs = (refs[0], refs[1:]) if closes else (None, refs)
    refs = refs[GROUP:]
    (image_ref, weight_ref), refs = (refs[:2], refs[2:]) if closes else ((None, None), refs)
    sums, (scaled, shifted, sems), refs = refs[:GROUP], refs[GROUP : GROUP + 3], refs[GROUP + 3 :]
    stage, refs = (refs[0], refs[1:]) if closes else (None, refs)
    count = pairs[0].shape[0] // 2
    me = own_index()
    begin = first // LANES
    used = parts - begin
    sources = 2 * chips
    tables = {(n, begin + p): refs[n * used + p] for n in range(sources) for p in range(used)}
    copies = []
    if closes:
        copies.append(pltpu.make_async_copy(weight_in, weight_ref, sems.at[len(tables)]))
        copies[0].start()
    for k, (n, p) in enumerate(tables):
        shifted[k] = spots[(me ^ (2 * low + n)) * parts + p] + (GROUP - n % GROUP)
    for k, table in enumerate(tables.values()):
        copies.append(pltpu.make_async_copy(shifted.at[pl.ds(k, 1)], table, sems.at[k]))
        copies[-1].start()
    for n in range(sources):
        turn, member = divmod(n, GROUP)
        rows = pairs[n // 2][n % 2 * count : (n % 2 + 1) * count, :].astype(f32)
        scaled[pl.ds(turn * count * GROUP + member, count, stride=GROUP), :] = rows * factors[me ^ (2 * low + n)]
    for copy in copies:
        copy.wait()
    add_rows(tables, scaled, sums, sources // GROUP, count, first)
    if not closes:
        return
    weight = weight_in[...]

    inverse = 1.0 / jnp.maximum(weight, 1.0)

    def mean(h, total):
        return total * jnp.broadcast_to(inverse[h : h + 1, :], (LANES, LANES)).T

    merge(sums, stage, mean, image_ref, sems)


def merge(sums, stage, finish, out_ref, sems):
    copies = []
    blocks = stage.shape[0] // LANES
    quarter = blocks // 4
    for h in range(blocks):
        total = [acc[GROUP + h * LANES : GROUP + (h + 1) * LANES, :] for acc in sums]
        while len(total) > 1:
            total = [a + b for a, b in zip(total[::2], total[1::2])] + total[len(total) // 2 * 2 :]
        stage[h * LANES : (h + 1) * LANES, :] = finish(h, total[0])
        if h % quarter == quarter - 1:
            ready = pl.ds((h + 1 - quarter) * LANES, quarter * LANES)
            copies.append(pltpu.make_async_copy(stage.at[ready], out_ref.at[ready], sems.at[h // quarter]))
            copies[-1].start()
    for copy in copies:
        copy.wait()


def body(raw_pixels, kernel_bank, kernel_ids, inv_var, gap_start, warp_tile, warp_offset):
    _, rows, cols = raw_pixels.shape
    segs = cols // LANES
    axes = ("expo", "fp")
    devices = lax.axis_size("expo") * lax.axis_size("fp")
    pieces = rows * segs
    capacity = 2 * pieces // devices
    parts = -(-capacity // LANES)
    slots = pieces

    raw = raw_pixels[0]
    above, below = halo(raw, "fp")
    tiles = jnp.transpose(warp_tile[0], (1, 2, 0))
    offsets = jnp.transpose(warp_offset[0], (1, 0))
    tall = -(-(rows + 2 * EDGE) // LANES) * LANES
    dest, meta, tv, th = pl.pallas_call(
        functools.partial(route_kernel, capacity),
        out_shape=(
            pltpu.VMEM((pieces // LANES, 1, LANES), i32),
            pltpu.VMEM((devices * META, LANES), bf16),
            pltpu.VMEM((rows, tall), bf16),
            pltpu.VMEM((2 * LANES, 4 * LANES), bf16),
        ),
        in_specs=[VMEM] * 6,
        out_specs=(VMEM,) * 4,
        scratch_shapes=[pltpu.VMEM((2, 4 * LANES), f32)],
        cost_estimate=cost(400_000_000, 600_000),
        compiler_params=params(16),
        name="route",
    )(far(tiles), far(offsets), gap_start, inv_var, kernel_ids, far(kernel_bank))

    capacity1 = capacity // 2
    capacity0 = capacity - capacity1
    chips = devices // 2
    everything, keep, give = pl.pallas_call(
        pack_kernel,
        out_shape=(pltpu.HBM((devices, capacity0 + META, LANES), bf16),)
        + (pltpu.VMEM((chips, capacity1, LANES), bf16),) * 2,
        in_specs=[ANY, ANY, ANY, VMEM, VMEM, VMEM, VMEM],
        out_specs=(ANY, VMEM, VMEM),
        scratch_shapes=[
            pltpu.VMEM((rows + 2 * EDGE, cols), bf16),
            pltpu.VMEM((rows, cols + 2 * LANES), bf16),
            pltpu.VMEM((pieces, LANES), f32),
            pltpu.VMEM((devices * capacity + 8, LANES), f32),
            pltpu.VMEM((devices, capacity0 + META, LANES), bf16),
            pltpu.SemaphoreType.DMA((3 + pieces // LANES,)),
        ]
        + [pltpu.SMEM((1, 1, LANES), i32)] * (pieces // LANES),
        cost_estimate=cost(10_000_000_000, 4_000_000),
        compiler_params=params(20),
        name="pack",
    )(far(raw), near(above), near(below), near(tv), near(th), near(dest), near(meta))

    most = 8 * devices
    total = pltpu.VMEM((-(-(slots + 3 * GROUP) // most) * most, LANES), f32)
    got = lax.all_to_all(everything, axes, split_axis=0, concat_axis=0, tiled=True)
    take = lax.ppermute(give, axes, [(i, i ^ 1) for i in range(devices)])
    joined = pl.pallas_call(
        join_kernel,
        out_shape=(pltpu.VMEM((2 * capacity1, LANES), bf16),) * chips,
        in_specs=[VMEM, VMEM],
        out_specs=(VMEM,) * chips,
        cost_estimate=cost(1_000_000, 1_000_000),
        compiler_params=params(2),
        name="join",
    )(near(keep), near(take))
    rest = [joined[0]]
    cuts = (0, chips // 2, chips * 3 // 4, chips)
    for low, high in zip(cuts, cuts[1:]):
        for j in range(max(low, 1), high):
            rest.append(lax.ppermute(joined[j], axes, [(i, i ^ (2 * j)) for i in range(devices)]))

    used = -(-capacity0 // LANES)
    spots, factors, weight, *sums = pl.pallas_call(
        functools.partial(first_kernel, slots, parts),
        out_shape=(
            pltpu.VMEM((devices * parts, 1, LANES), i32),
            pltpu.VMEM((devices, 1, LANES), f32),
            pltpu.VMEM((slots // LANES, LANES), f32),
        )
        + (total,) * GROUP,
        in_specs=[VMEM],
        out_specs=(VMEM,) * (3 + GROUP),
        scratch_shapes=[
            pltpu.VMEM((devices * capacity0, LANES), f32),
            pltpu.VMEM((devices * used, 1, LANES), i32),
            pltpu.SemaphoreType.DMA((devices * used,)),
        ]
        + [pltpu.SMEM((1, 1, LANES), i32)] * (devices * used),
        cost_estimate=cost(4_000_000_000, 8_000_000),
        compiler_params=params(8),
        name="sum_first",
    )(near(got))
    used = parts - capacity0 // LANES
    for low, high in zip(cuts, cuts[1:]):
        closes = high == chips
        number, here = high - low, 2 * (high - low)
        ends = (pltpu.HBM((slots, LANES), f32), pltpu.HBM((slots // LANES, LANES), f32)) if closes else ()
        lead = number + 2 + closes
        out = pl.pallas_call(
            functools.partial(rest_kernel, low, high, capacity0, parts, closes),
            out_shape=ends + (total,) * GROUP,
            in_specs=[VMEM] * (lead + GROUP),
            out_specs=(ANY,) * len(ends) + (VMEM,) * GROUP,
            scratch_shapes=[
                pltpu.VMEM((here * capacity1, LANES), f32),
                pltpu.VMEM((here * used, 1, LANES), i32),
                pltpu.SemaphoreType.DMA((here * used + 1,)),
            ]
            + [pltpu.VMEM((slots, LANES), f32)] * closes
            + [pltpu.SMEM((1, 1, LANES), i32)] * (here * used),
            input_output_aliases={lead + k: len(ends) + k for k in range(GROUP)},
            cost_estimate=cost(4_000_000_000, 8_000_000),
            compiler_params=params(8),
        )(
            *[near(x) for x in rest[low:high]],
            near(spots),
            near(factors),
            *[near(weight)] * closes,
            *[near(x) for x in sums],
        )
        sums = out[len(ends) :]
    image, weight = out[:2]
    return image[None], weight.reshape(1, slots)


def solution(mesh):
    in_specs = (
        P("expo", "fp", None),
        P(),
        P("expo", "fp"),
        P("expo", "fp"),
        P("expo", "fp"),
        P("expo", "fp", None, None),
        P("expo", "fp", None),
    )
    out_specs = (P(("expo", "fp"), None, None), P(("expo", "fp"), None))
    return jax.shard_map(body, mesh=mesh, in_specs=in_specs, out_specs=out_specs, check_vma=False)
```
